256 devices in a mesh: row: 16 (over z_lo, x, core), col: 16 (over y, z_hi).
Axes of the slice: x: 4, y: 4, z: 8 (z_hi: 4, z_lo: 2; z = z_hi * 2 + z_lo), core: 2. Of those that a mesh axis runs over, the one named last changes fastest.
Arguments:
- matrix_tiles: float32 [1, 16, 1, 16, 1024, 1024], P(None, 'row', None, 'col'), may hold values from -17 to 17, as said below
- panels: float32 [3, 1, 16, 512, 128], P(None, None, 'row', 'col'), may hold values from -0.25 to 0.25
- plan: int32 [3, 16], replicated, may hold values 0 or 1
Outputs:
- updated_tiles: float32 [1, 16, 1, 16, 1024, 1024], P(None, 'row', None, 'col')
The draws below stay inside these ranges and needn't reach their ends.
Inputs may be any that keep to these rules, and one draw needn't show every extreme that they name: `matrix_tiles`: entries below the first subdiagonal of the matrix are zero.
All inputs are finite; a program needn't handle non-finite values.
Results may differ from the reference program's by a relative error of at most 0.0003.
Values sent between devices are 32-bit elements; how exact they have to be, the bound alone decides.
A program may use at most 64 MiB of HBM per device.

```python
import jax
import jax.numpy as jnp
from jax import lax

TILE = 1024
WIN = 512
REFL = 128
ROUNDS = 3
NT = 16
N_ROW = 16
N_COL = 16


def draw_matrix_tiles(key, part):
    matrix_order = NT * TILE
    values = jax.random.truncated_normal(jax.random.fold_in(key, 7), -6.0, 6.0, (matrix_order, matrix_order), jnp.float32)
    row_index = lax.broadcasted_iota(jnp.int32, (matrix_order, matrix_order), 0)
    col_index = lax.broadcasted_iota(jnp.int32, (matrix_order, matrix_order), 1)
    values = jnp.where(row_index <= col_index + 1, values, 0.0)
    return values.reshape(NT // N_ROW, N_ROW, TILE, NT // N_COL, N_COL, TILE).transpose(0, 1, 3, 4, 2, 5)


def touch_ends(drawn, own_key, least, top_value):
    place = [jax.random.randint(jax.random.fold_in(own_key, axis), (), 0, length) for axis, length in enumerate(drawn.shape)]
    longest = drawn.shape.index(max(drawn.shape))
    neighbour = place[:longest] + [(place[longest] + 1) % drawn.shape[longest]] + place[longest + 1:]
    return drawn.at[tuple(place)].set(least).at[tuple(neighbour)].set(top_value)


def block_levels(key, dims, shards, low, top_value):
    factor_of, own = 1.0, jax.random.fold_in(key, 6)
    for axis_at, shards_of in shards:
        heights = jnp.exp(jax.random.uniform(jax.random.fold_in(own, axis_at), (shards_of,), jnp.float32, low / len(shards), top_value / len(shards)))
        factor_of = factor_of * jnp.repeat(heights, dims[axis_at] // shards_of).reshape([-1 if axis == axis_at else 1 for axis in range(len(dims))])
    return factor_of


def centred(stream_key, extent, scale, most, pieces=(), kind=jnp.bfloat16):
    gain = block_levels(stream_key, extent, pieces, -0.22, 0.18) if pieces else 1.0
    array = jax.random.normal(stream_key, extent, jnp.float32) * scale * gain
    return jnp.minimum(jnp.maximum(array, -most), most).astype(kind)


def setup_inputs(seed: int = 0) -> dict:
    seeds = jax.random.split(jax.random.key(seed), 4)
    return {
        "matrix_tiles": draw_matrix_tiles(jax.random.fold_in(seeds[3], 71), 0),
        "panels": centred(seeds[1], (ROUNDS, NT // N_ROW, N_ROW, WIN, REFL), WIN ** -0.5, 0.25, ((2, 16), (3, 16)), jnp.float32),
        "plan": touch_ends((jax.random.randint(seeds[2], (ROUNDS, NT), 0, 4) < 3).astype(jnp.int32), jax.random.fold_in(seeds[2], 1), 0, 1),
    }


exact_mode = lax.Precision.HIGHEST


def round_offsets(tile_size, window):
    return [0, tile_size - window // 2, window // 2]


def upper_inverse(upper_part):
    order_n = upper_part.shape[0]
    identity = jnp.eye(order_n, dtype=upper_part.dtype)
    scale = 1.0 / jnp.diag(upper_part)
    power = identity - upper_part * scale[:, None]
    result = identity + power
    span = 2
    while span < order_n:
        power = jnp.dot(power, power, precision=exact_mode)
        result = jnp.dot(result, identity + power, precision=exact_mode)
        span = span * 2
    return result * scale[None, :]


def window_factor(reflect):
    window, reflectors = reflect.shape
    gram_matrix = jnp.dot(reflect.T, reflect, precision=exact_mode)
    upper_part = jnp.triu(gram_matrix, 1) + jnp.diag(jnp.diag(gram_matrix) * 0.5)
    factor = upper_inverse(upper_part)
    product = jnp.dot(reflect, factor, precision=exact_mode)
    return jnp.eye(window, dtype=reflect.dtype) - jnp.dot(product, reflect.T, precision=exact_mode)


def reference(matrix_tiles, panels, plan):
    matrix_order = NT * TILE
    hessen = matrix_tiles.transpose(0, 1, 4, 2, 3, 5).reshape(matrix_order, matrix_order)
    reflect_all = panels.reshape(ROUNDS, NT, WIN, REFL)
    identity = jnp.eye(WIN, dtype=panels.dtype)
    tile_ids = jnp.arange(NT, dtype=jnp.int32)
    offsets = round_offsets(TILE, WIN)
    for round_at in range(ROUNDS):
        offset = offsets[round_at]
        factors = lax.map(window_factor, reflect_all[round_at])
        active = plan[round_at] > 0
        windows = NT
        if offset + WIN > TILE:
            active = jnp.logical_and(active, tile_ids < NT - 1)
            windows = NT - 1
        factors = jnp.where(active[:, None, None], factors, identity)

        def left_step(window_at, matrix, factors=factors, offset=offset):
            start_at = (window_at * TILE + offset).astype(jnp.int32)
            zero_at = jnp.zeros((), jnp.int32)
            rows_block = lax.dynamic_slice(matrix, (start_at, zero_at), (WIN, matrix_order))
            factor = factors[window_at]
            return lax.dynamic_update_slice(matrix, jnp.dot(factor.T, rows_block, precision=exact_mode), (start_at, zero_at))

        def right_step(window_at, matrix, factors=factors, offset=offset):
            start_at = (window_at * TILE + offset).astype(jnp.int32)
            zero_at = jnp.zeros((), jnp.int32)
            cols_block = lax.dynamic_slice(matrix, (zero_at, start_at), (matrix_order, WIN))
            factor = factors[window_at]
            return lax.dynamic_update_slice(matrix, jnp.dot(cols_block, factor, precision=exact_mode), (zero_at, start_at))

        hessen = lax.fori_loop(0, windows, left_step, hessen)
        hessen = lax.fori_loop(0, windows, right_step, hessen)
    return hessen.reshape(NT // N_ROW, N_ROW, TILE, NT // N_COL, N_COL, TILE).transpose(0, 1, 3, 4, 2, 5)
```

```python
import functools

import jax
import jax.numpy as jnp
from jax import lax
from jax.experimental import pallas as pl
from jax.experimental.pallas import tpu as pltpu
from jax.sharding import PartitionSpec as P

MESH = pl.DeviceIdType.MESH
F32 = jnp.float32
BF16 = jnp.bfloat16

X_N, CORE_N, Y_N, ZH_N = 4, 2, 4, 4
CHUNKS = 8
MAX_DEPTH = 4


def split(value):
    high = value.astype(BF16)
    low = (value - high.astype(F32)).astype(BF16)
    return high, low


def dot3(left, right, turned=False):
    dims = (((1,), (1 if turned else 0,)), ((), ()))

    def one(a, b):
        return lax.dot_general(a, b, dims, preferred_element_type=F32)

    return one(left[0], right[0]) + (one(left[0], right[1]) + one(left[1], right[0]))


def exact_dot(left, right):
    return jnp.dot(left, right, precision=lax.Precision.HIGHEST, preferred_element_type=F32)


def kernel(
    rows_n, cols_n, b, h_ref, panel_ref, plan_ref, out_ref,
    pack_l, pack_r, tile, high, low, pair_h, pair_l, thin_h, thin_l, turn_h, turn_l, tthin_h, tthin_l,
    f_h, f_l, ft_h, ft_l, cc_h, cc_l, u0_h, u0_l, t_own, p_own, from_below, from_above,
    st_own, sb_own, from_right, from_left, y0_h, y0_l,
    h_sem, out_sem, g_send, g_recv, y_send, y_recv, f_send, f_recv, n_send, n_recv,
    tree_send, tree_recv, up_send, up_recv, dn_send, dn_recv, rt_send, rt_recv, lf_send, lf_recv,
):
    h = b // 2
    piece = 2 * b // cols_n
    r = lax.axis_index("row")
    c = lax.axis_index("col")
    zl, x, core = r // (X_N * CORE_N), (r // CORE_N) % X_N, r % CORE_N
    y, zh = c // ZH_N, c % ZH_N

    def row_of(zl, x, core):
        return zl * (X_N * CORE_N) + x * CORE_N + core

    def col_of(y, zh):
        return y * ZH_N + zh

    active = r <= c + 1
    has_up = jnp.logical_and(active, r > 0)
    has_dn = jnp.logical_and(r < rows_n - 1, r <= c)
    has_rt = jnp.logical_and(active, c < cols_n - 1)
    has_lf = jnp.logical_and(r <= c, c > 0)

    up_dev, dn_dev = (r - 1, c), (r + 1, c)
    rt_dev, lf_dev = (r, c + 1), (r, c - 1)
    zh_dev = [(r, col_of(y, (zh + d) % ZH_N)) for d in (1, 2, 3)]
    y_up, y_dn = (y + 1) % Y_N, (y + Y_N - 1) % Y_N
    y_dev = [(r, col_of(y_up, zh)), (r, col_of(y_dn, zh))]
    core_dev = (row_of(zl, x, 1 - core), c)
    z_dev = (row_of(1 - zl, x, core), c)
    xp_dev = (row_of(zl, (x + 1) % X_N, core), c)
    xm_dev = (row_of(zl, (x + X_N - 1) % X_N, core), c)

    def remote(src, dst, send, recv, device):
        return pltpu.make_async_remote_copy(
            src_ref=src, dst_ref=dst, send_sem=send, recv_sem=recv, device_id=device, device_id_type=MESH
        )

    def tile_in(j):
        return pltpu.make_async_copy(h_ref.at[:, pl.ds(j * b, b)], tile.at[j], h_sem.at[j])

    for j in range(4):
        tile_in(j).start()

    barrier = pltpu.get_barrier_semaphore()
    around = [((r + step) % rows_n, c) for step in (1, rows_n - 1)] + [(r, (c + step) % cols_n) for step in (1, cols_n - 1)]
    peers = zh_dev + y_dev + [core_dev, z_dev, xp_dev, xm_dev] + around
    for device in peers:
        pl.semaphore_signal(barrier, inc=1, device_id=device, device_id_type=MESH)
    pl.semaphore_wait(barrier, len(peers))

    def place(k, col):
        if k == 0:
            return col * piece
        if k == 2:
            return 2 * b + col * piece
        return 4 * b + col * piece + (col // (cols_n // 2)) * (3 * b)

    def rows(k, col, skip, count):
        start = pl.multiple_of(place(k, col) + skip, 2 * piece if count > piece else piece)
        return pack_l.at[pl.ds(start, count)]

    def z_copy(d, k, col):
        return remote(panel_ref.at[k], rows(k, col, 0, piece), g_send.at[d, k], g_recv.at[d, k], zh_dev[d])

    order = (0, 2, 1)
    for k in order:
        for d in range(3):
            z_copy(d, k, c).start()
        pack_l[pl.ds(pl.multiple_of(place(k, c), piece), piece), :] = panel_ref[k]

    @pl.when(jnp.logical_not(has_dn))
    def _():
        from_below[...] = jnp.zeros_like(from_below)

    @pl.when(jnp.logical_not(has_up))
    def _():
        from_above[...] = jnp.zeros_like(from_above)
        pack_l[5 * b : 6 * b, :] = jnp.zeros((b, h), F32)
        pack_l[7 * b + h : 8 * b, :] = jnp.zeros((h, h), F32)

    @pl.when(jnp.logical_not(has_rt))
    def _():
        from_right[...] = jnp.zeros_like(from_right)

    @pl.when(jnp.logical_not(has_lf))
    def _():
        from_left[...] = jnp.zeros_like(from_left)

    def y_copy(side, k, at_y):
        block = rows(k, col_of(at_y, 0), 0, 4 * piece)
        return remote(block, block, y_send.at[side, k], y_recv.at[side, k], y_dev[side])

    def pass_copy(side, k, at_y):
        block = rows(k, col_of(at_y, 0), side * 2 * piece, 2 * piece)
        return remote(block, block, f_send.at[side, k], f_recv.at[side, k], y_dev[side])

    for k in order:
        for d in range(3):
            z_copy(d, k, col_of(y, (zh + ZH_N - 1 - d) % ZH_N)).wait_recv()
        for side in range(2):
            y_copy(side, k, y).start()
    sources = (y_dn, y_up)
    for k in order:
        for side in range(2):
            y_copy(side, k, sources[side]).wait_recv()
            pass_copy(side, k, sources[side]).start()

    for j in range(4):
        tile_in(j).wait()

    @pl.when(active)
    def _():
        @pl.loop(0, 4)
        def _(j):
            @pl.loop(0, 4)
            def _(i):
                at = pl.ds(pl.multiple_of(i * b, b), b)
                part_h, part_l = split(tile[j, at, :])
                high[j, at, :] = part_h
                low[j, at, :] = part_l

    far = (y + 2) % Y_N
    for k in order:
        for side in range(2):
            pass_copy(side, k, far).wait_recv()

    def bottom_copy():
        return remote(pack_l.at[8 * b : 9 * b], pack_l.at[5 * b : 6 * b], n_send.at[0], n_recv.at[0], dn_dev)

    def factor_copy():
        return remote(
            pack_l.at[6 * b + h : 7 * b], pack_l.at[7 * b + h : 8 * b], n_send.at[1], n_recv.at[1], dn_dev
        )

    root_zl, root_x, root_core = c // (X_N * CORE_N), (c // CORE_N) % X_N, c % CORE_N
    dx = (x + X_N - root_x) % X_N
    dz = jnp.where(zl == root_zl, 0, 1)
    dc = jnp.where(core == root_core, 0, 1)
    depth = dz + dc + jnp.where(dx == 0, 0, jnp.where(dx == 2, 2, 1))
    own = dc == 0
    is_root = r == c

    def children(q):
        even = q % 2 == 0
        odd = q % 2 == 1
        return [
            (jnp.logical_and(own, jnp.logical_or(dx == 0, jnp.logical_and(dx == 1, even))), xp_dev),
            (jnp.logical_and(own, jnp.logical_or(dx == 0, jnp.logical_and(dx == 3, odd))), xm_dev),
            (is_root, z_dev),
            (own, core_dev),
        ]

    def chunk(ref, q):
        return ref.at[pl.ds(pl.multiple_of(q * b, b), b)]

    def tree_copy(source, q, child, device):
        return remote(chunk(source, q), chunk(pack_r, q), tree_send.at[child, q], tree_recv.at[q], device)

    def hand_down(source, q):
        for child, (wanted, device) in enumerate(children(q)):

            @pl.when(wanted)
            def _():
                tree_copy(source, q, child, device).start()

    def poll(p):
        q = p - depth

        @pl.when(jnp.logical_and(depth > 0, jnp.logical_and(q >= 0, q < CHUNKS)))
        def _():
            at = jnp.clip(q, 0, CHUNKS - 1)
            tree_copy(pack_r, at, 0, core_dev).wait_recv()
            hand_down(pack_r, at)

    @pl.when(is_root)
    def _():
        @pl.loop(0, 5)
        def _(q):
            hand_down(pack_l, q)

    @pl.when(has_dn)
    def _():
        bottom_copy().start()

    def keep_f(slot, value):
        part_h, part_l = split(value)
        f_h[slot], f_l[slot] = part_h, part_l

    def keep_ft(slot, value):
        part_h, part_l = split(value.T)
        ft_h[slot], ft_l[slot] = part_h, part_l

    @pl.when(active)
    def _():
        at_row = lax.broadcasted_iota(jnp.int32, (h, h), 0)
        at_col = lax.broadcasted_iota(jnp.int32, (h, h), 1)
        eye = jnp.where(at_row == at_col, 1.0, 0.0).astype(F32)
        panels = [[pack_l[0 : 2 * b, :]], [pack_l[4 * b : 5 * b, :], pack_l[8 * b : 9 * b, :]], [pack_l[2 * b : 4 * b, :]]]
        powers, results, scales = [], [], []
        for parts in panels:
            gram = sum(exact_dot(part.T, part) for part in parts)
            upper = jnp.where(at_row < at_col, gram, jnp.where(at_row == at_col, gram * 0.5, 0.0))
            diag = jnp.where(at_row == at_col, upper, 0.0)
            power = eye - upper * (1.0 / jnp.sum(diag, axis=1, keepdims=True))
            powers.append(power)
            results.append(eye + power)
            scales.append(1.0 / jnp.sum(diag, axis=0, keepdims=True))
        span = 2
        while span < h:
            powers = [exact_dot(power, power) for power in powers]
            results = [result + exact_dot(result, power) for result, power in zip(results, powers)]
            span = span * 2
        live = [
            plan_ref[0, r] > 0,
            jnp.logical_and(plan_ref[1, r] > 0, r < rows_n - 1),
            plan_ref[2, r] > 0,
        ]
        for k in range(3):
            factor = jnp.where(live[k], results[k] * scales[k], 0.0)
            pack_l[6 * b + k * h : 6 * b + (k + 1) * h, :] = factor
            keep_ft(k, factor)

    @pl.when(has_dn)
    def _():
        factor_copy().start()

    poll(1)

    @pl.when(has_up)
    def _():
        bottom_copy().wait_recv()

    @pl.when(is_root)
    def _():
        hand_down(pack_l, 5)

    poll(2)

    def operators(pack):
        pairs = [
            jnp.concatenate([pack[0:b, :], pack[5 * b : 6 * b, :]], axis=1),
            jnp.concatenate([pack[b : 2 * b, :], pack[2 * b : 3 * b, :]], axis=1),
        ]
        thin = [pack[3 * b : 4 * b, :], pack[4 * b : 5 * b, :]]
        for at in range(2):
            pair_h[at], pair_l[at] = split(pairs[at])
            thin_h[at], thin_l[at] = split(thin[at])
        first = exact_dot(pack[5 * b : 6 * b, :].T, pack[0:b, :])
        second = exact_dot(pack[2 * b : 3 * b, :].T, pack[b : 2 * b, :])
        cc_h[...], cc_l[...] = split(jnp.concatenate([first, second], axis=0))
        return pairs, thin

    def pair(at):
        return pair_h[at], pair_l[at]

    def thinner(at):
        return thin_h[at], thin_l[at]

    def turned(at):
        return turn_h[at], turn_l[at]

    def tthin(at):
        return tthin_h[at], tthin_l[at]

    def part(col, at):
        return high[col, at, :], low[col, at, :]

    def keep(col, at, value):
        tile[col, at, :] = value
        high[col, at, :], low[col, at, :] = split(value)

    band = [slice(i * b, (i + 1) * b) for i in range(4)]

    def t_copy(j):
        return remote(t_own.at[j], from_above.at[j], dn_send.at[j], dn_recv.at[j], dn_dev)

    def p_copy(j):
        return remote(p_own.at[j], from_below.at[j], up_send.at[j], up_recv.at[j], up_dev)

    @pl.when(active)
    def _():
        pairs, thin = operators(pack_l)
        for at in range(2):
            turn_h[at], turn_l[at] = split(pairs[at].T)
            tthin_h[at], tthin_l[at] = split(thin[at].T)

    @pl.loop(0, 4)
    def _(j):
        @pl.when(active)
        def _():
            x0 = dot3(turned(0), part(j, band[0]))
            x1 = dot3(turned(1), part(j, band[1]))
            x2 = dot3(tthin(0), part(j, band[2]))
            t_own[j] = dot3(tthin(1), part(j, band[3]))
            u0 = split(dot3((ft_h[0], ft_l[0]), split(x0[:h] + x1[:h])))
            u0_h[j], u0_l[j] = u0
            shift = dot3((cc_h[...], cc_l[...]), u0)
            p_own[j] = x0[h:] - shift[:h]

            @pl.when(has_dn)
            def _():
                t_copy(j).start()

            @pl.when(has_up)
            def _():
                p_copy(j).start()

            u2 = split(dot3((ft_h[2], ft_l[2]), split(x1[h:] + x2 - shift[h:])))
            both = tuple(jnp.concatenate([a, z], axis=0) for a, z in zip(u0, u2))
            keep(j, band[1], tile[j, band[1], :] - dot3(pair(1), both))
            keep(j, band[2], tile[j, band[2], :] - dot3(thinner(0), u2))

        poll(3 + j)

    @pl.when(has_up)
    def _():
        factor_copy().wait_recv()

    @pl.when(active)
    def _():
        keep_ft(3, pack_l[7 * b + h : 8 * b, :])

    @pl.when(is_root)
    def _():
        hand_down(pack_l, 6)
        hand_down(pack_l, 7)
        pack_r[...] = pack_l[0 : 8 * b, :]

    @pl.loop(0, 4)
    def _(j):
        @pl.when(has_dn)
        def _():
            p_copy(j).wait_recv()

        @pl.when(has_up)
        def _():
            t_copy(j).wait_recv()

        @pl.when(active)
        def _():
            u1 = split(dot3((ft_h[1], ft_l[1]), split(t_own[j] + from_below[j])))
            u1p = split(dot3((ft_h[3], ft_l[3]), split(from_above[j] + p_own[j])))
            both = tuple(jnp.concatenate([a, z], axis=0) for a, z in zip((u0_h[j], u0_l[j]), u1p))
            keep(j, band[0], tile[j, band[0], :] - dot3(pair(0), both))
            keep(j, band[3], tile[j, band[3], :] - dot3(thinner(1), u1))

        poll(7 + j)

    poll(11)
    poll(12)

    def st_copy(i):
        return remote(st_own.at[i], from_left.at[i], rt_send.at[i], rt_recv.at[i], rt_dev)

    def sb_copy(i):
        return remote(sb_own.at[i], from_right.at[i], lf_send.at[i], lf_recv.at[i], lf_dev)

    def out_copy(i, j):
        at = pl.ds(pl.multiple_of(i * b, b), b)
        return pltpu.make_async_copy(tile.at[j, at], out_ref.at[at, pl.ds(j * b, b)], out_sem.at[i, j])

    @pl.when(active)
    def _():
        operators(pack_r)
        for k in range(4):
            keep_f(k, pack_r[6 * b + k * h : 6 * b + (k + 1) * h, :])

    def f_of(k):
        return f_h[k], f_l[k]

    @pl.when(active)
    def _():
        @pl.loop(0, 4)
        def _(i):
            at = pl.ds(pl.multiple_of(i * b, b), b)
            x0 = dot3(part(0, at), pair(0))
            x1 = dot3(part(1, at), pair(1))
            x2 = dot3(part(2, at), thinner(0))
            st_own[i] = dot3(part(3, at), thinner(1))
            y0 = split(dot3(split(x0[:, :h] + x1[:, :h]), f_of(0)))
            y0_h[i], y0_l[i] = y0
            shift = dot3(y0, (cc_h[...], cc_l[...]), turned=True)
            sb_own[i] = x0[:, h:] - shift[:, :h]

            @pl.when(has_rt)
            def _():
                st_copy(i).start()

            @pl.when(has_lf)
            def _():
                sb_copy(i).start()

            y2 = split(dot3(split(x1[:, h:] + x2 - shift[:, h:]), f_of(2)))
            both = tuple(jnp.concatenate([a, z], axis=1) for a, z in zip(y0, y2))
            tile[1, at, :] = tile[1, at, :] - dot3(both, pair(1), turned=True)
            tile[2, at, :] = tile[2, at, :] - dot3(y2, thinner(0), turned=True)

    @pl.loop(0, 4)
    def _(i):
        @pl.when(has_rt)
        def _():
            sb_copy(i).wait_recv()

        @pl.when(has_lf)
        def _():
            st_copy(i).wait_recv()

        @pl.when(active)
        def _():
            at = pl.ds(pl.multiple_of(i * b, b), b)
            y1 = split(dot3(split(st_own[i] + from_right[i]), f_of(1)))
            y1p = split(dot3(split(from_left[i] + sb_own[i]), f_of(3)))
            both = tuple(jnp.concatenate([a, z], axis=1) for a, z in zip((y0_h[i], y0_l[i]), y1p))
            tile[0, at, :] = tile[0, at, :] - dot3(both, pair(0), turned=True)
            tile[3, at, :] = tile[3, at, :] - dot3(y1, thinner(1), turned=True)

        for j in range(4):
            out_copy(i, j).start()

    for k in range(3):
        for d in range(3):
            z_copy(d, k, c).wait_send()
        for side in range(2):
            y_copy(side, k, y).wait_send()
            pass_copy(side, k, sources[side]).wait_send()

    @pl.when(has_dn)
    def _():
        bottom_copy().wait_send()
        factor_copy().wait_send()

    @pl.loop(0, CHUNKS)
    def _(q):
        for child, (wanted, device) in enumerate(children(q)):

            @pl.when(wanted)
            def _():
                tree_copy(pack_r, q, child, device).wait_send()

    @pl.loop(0, 4)
    def _(j):
        for there, copy in ((has_dn, t_copy), (has_up, p_copy), (has_rt, st_copy), (has_lf, sb_copy)):

            @pl.when(there)
            def _():
                copy(j).wait_send()

        for k in range(4):
            out_copy(j, k).wait()


def solution(mesh):
    rows_n, cols_n = mesh.shape["row"], mesh.shape["col"]

    def on_device(matrix_tiles, panels, plan):
        size, refl = matrix_tiles.shape[-1], panels.shape[-1]
        b, h = size // 4, refl
        piece = panels.shape[3]
        vmem, dma = pltpu.VMEM, pltpu.SemaphoreType.DMA
        scratch = [
            vmem((9 * b, h), F32), vmem((8 * b, h), F32), vmem((4, size, b), F32),
            vmem((4, size, b), BF16), vmem((4, size, b), BF16),
            vmem((2, b, b), BF16), vmem((2, b, b), BF16), vmem((2, b, h), BF16), vmem((2, b, h), BF16),
            vmem((2, b, b), BF16), vmem((2, b, b), BF16), vmem((2, h, b), BF16), vmem((2, h, b), BF16),
            vmem((4, h, h), BF16), vmem((4, h, h), BF16), vmem((4, h, h), BF16), vmem((4, h, h), BF16),
            vmem((b, h), BF16), vmem((b, h), BF16), vmem((4, h, b), BF16), vmem((4, h, b), BF16),
            vmem((4, h, b), F32), vmem((4, h, b), F32), vmem((4, h, b), F32), vmem((4, h, b), F32),
            vmem((4, b, h), F32), vmem((4, b, h), F32), vmem((4, b, h), F32), vmem((4, b, h), F32),
            vmem((4, b, h), BF16), vmem((4, b, h), BF16),
            dma((4,)), dma((4, 4)), dma((3, 3)), dma((3, 3)), dma((2, 3)), dma((2, 3)), dma((2, 3)), dma((2, 3)),
            dma((2,)), dma((2,)), dma((4, CHUNKS)), dma((CHUNKS,)),
            dma((4,)), dma((4,)), dma((4,)), dma((4,)), dma((4,)), dma((4,)), dma((4,)), dma((4,)),
        ]
        result = pl.pallas_call(
            functools.partial(kernel, rows_n, cols_n, b),
            out_shape=jax.ShapeDtypeStruct((size, size), F32),
            in_specs=[
                pl.BlockSpec(memory_space=pl.ANY),
                pl.BlockSpec(memory_space=pltpu.VMEM),
                pl.BlockSpec(memory_space=pltpu.SMEM),
            ],
            out_specs=pl.BlockSpec(memory_space=pl.ANY),
            scratch_shapes=scratch,
            compiler_params=pltpu.CompilerParams(
                collective_id=0, has_side_effects=True, vmem_limit_bytes=40 * 1024 * 1024
            ),
        )(matrix_tiles.reshape(size, size), panels.reshape(3, piece, refl), plan)
        return result.reshape(matrix_tiles.shape)

    placed = (P(None, "row", None, "col", None, None), P(None, None, "row", "col", None), P())
    return jax.shard_map(
        on_device,
        mesh=mesh,
        in_specs=placed,
        out_specs=P(None, "row", None, "col", None, None),
        check_vma=False,
    )
```

```python
import functools

import jax
import jax.numpy as jnp
from jax import lax
from jax.experimental import pallas as pl
from jax.experimental.pallas import tpu as pltpu
from jax.sharding import PartitionSpec as P

MESH = pl.DeviceIdType.MESH
F32 = jnp.float32
BF16 = jnp.bfloat16

X_N, CORE_N, Y_N, ZH_N = 4, 2, 4, 4
CHUNKS = 7


def split(value):
    high = value.astype(BF16)
    low = (value - high.astype(F32)).astype(BF16)
    return high, low


def dot3(left, right, turned=False):
    side = 1 if turned else 0
    a = jnp.concatenate([left[0], left[0], left[1]], axis=1)
    z = jnp.concatenate([right[0], right[1], right[0]], axis=side)
    return lax.dot_general(a, z, (((1,), (side,)), ((), ())), preferred_element_type=F32)


def join(first, second, axis):
    return tuple(jnp.concatenate([a, z], axis=axis) for a, z in zip(first, second))


def exact_dot(left, right):
    return jnp.dot(left, right, precision=lax.Precision.HIGHEST, preferred_element_type=F32)


def kernel(
    rows_n, cols_n, b, h_ref, panel_ref, plan_hbm, out_ref,
    plan_ref, pack_l, pack_r, tile, high, low, pair_h, pair_l, thin_h, thin_l, turn_h, turn_l, tthin_h, tthin_l,
    f_h, f_l, cc_h, cc_l, t0_h, t0_l, t2_own, u2_h, u2_l, t_own, p_own, from_below, from_above,
    st_own, sb_own, from_right, from_left, y0_h, y0_l,
    in_sem, own_sem, out_sem, g_send, g_recv, y_send, y_recv, f_send, f_recv, n_send, n_recv,
    tree_send, tree_recv, row_send, row_recv, rt_send, rt_recv, lf_send, lf_recv,
):
    h = b // 2
    piece = 2 * b // cols_n
    r = lax.axis_index("row")
    c = lax.axis_index("col")
    zl, x, core = r // (X_N * CORE_N), (r // CORE_N) % X_N, r % CORE_N
    y, zh = c // ZH_N, c % ZH_N

    def row_of(zl, x, core):
        return zl * (X_N * CORE_N) + x * CORE_N + core

    def col_of(y, zh):
        return y * ZH_N + zh

    active = r <= c + 1
    has_up = jnp.logical_and(active, r > 0)
    has_dn = jnp.logical_and(r < rows_n - 1, r <= c)
    has_rt = jnp.logical_and(active, c < cols_n - 1)
    has_lf = jnp.logical_and(r <= c, c > 0)

    up_dev, dn_dev = (r - 1, c), (r + 1, c)
    rt_dev, lf_dev = (r, c + 1), (r, c - 1)
    zh_dev = [(r, col_of(y, (zh + d) % ZH_N)) for d in (1, 2, 3)]
    y_up, y_dn = (y + 1) % Y_N, (y + Y_N - 1) % Y_N
    y_dev = [(r, col_of(y_up, zh)), (r, col_of(y_dn, zh))]
    core_dev = (row_of(zl, x, 1 - core), c)
    z_dev = (row_of(1 - zl, x, core), c)
    xp_dev = (row_of(zl, (x + 1) % X_N, core), c)
    xm_dev = (row_of(zl, (x + X_N - 1) % X_N, core), c)

    def remote(src, dst, send, recv, device):
        return pltpu.make_async_remote_copy(
            src_ref=src, dst_ref=dst, send_sem=send, recv_sem=recv, device_id=device, device_id_type=MESH
        )

    tile_in = pltpu.make_async_copy(h_ref, tile, in_sem.at[0])
    plan_in = pltpu.make_async_copy(plan_hbm, plan_ref, in_sem.at[1])
    plan_in.start()
    tile_in.start()

    barrier = pltpu.get_barrier_semaphore()
    around = [((r + step) % rows_n, c) for step in (1, rows_n - 1)] + [(r, (c + step) % cols_n) for step in (1, cols_n - 1)]
    peers = zh_dev + y_dev + [core_dev, z_dev, xp_dev, xm_dev] + around
    for device in peers:
        pl.semaphore_signal(barrier, inc=1, device_id=device, device_id_type=MESH)
    pl.semaphore_wait(barrier, len(peers))

    def place(k, col):
        if k == 0:
            return col * piece
        if k == 2:
            return 2 * b + col * piece
        return 4 * b + col * piece + (col // (cols_n // 2)) * (3 * b)

    def rows(k, col, skip, count):
        start = pl.multiple_of(place(k, col) + skip, 2 * piece if count > piece else piece)
        return pack_l.at[pl.ds(start, count)]

    def z_copy(d, k, col):
        return remote(panel_ref.at[k], rows(k, col, 0, piece), g_send.at[d, k], g_recv.at[d, k], zh_dev[d])

    def own_copy(k):
        return pltpu.make_async_copy(panel_ref.at[k], rows(k, c, 0, piece), own_sem.at[k])

    order = (0, 2, 1)
    for k in order:
        for d in range(3):
            z_copy(d, k, c).start()
        own_copy(k).start()

    @pl.when(jnp.logical_not(has_dn))
    def _():
        from_below[...] = jnp.zeros_like(from_below)

    @pl.when(jnp.logical_not(has_up))
    def _():
        from_above[...] = jnp.zeros_like(from_above)
        pack_l[5 * b : 6 * b, :] = jnp.zeros((b, h), F32)
        pack_l[7 * b + h : 8 * b, :] = jnp.zeros((h, h), F32)

    @pl.when(jnp.logical_not(has_rt))
    def _():
        from_right[...] = jnp.zeros_like(from_right)

    @pl.when(jnp.logical_not(has_lf))
    def _():
        from_left[...] = jnp.zeros_like(from_left)

    root_zl, root_x, root_core = c // (X_N * CORE_N), (c // CORE_N) % X_N, c % CORE_N
    dx = (x + X_N - root_x) % X_N
    dz = jnp.where(zl == root_zl, 0, 1)
    dc = jnp.where(core == root_core, 0, 1)
    depth = dz + dc + jnp.where(dx == 0, 0, jnp.where(dx == 2, 2, 1))
    own = dc == 0
    is_root = r == c

    def children(q):
        even = q % 2 == 0
        odd = q % 2 == 1
        return [
            (jnp.logical_and(own, jnp.logical_or(dx == 0, jnp.logical_and(dx == 1, even))), xp_dev),
            (jnp.logical_and(own, jnp.logical_or(dx == 0, jnp.logical_and(dx == 3, odd))), xm_dev),
            (is_root, z_dev),
            (own, core_dev),
        ]

    def units(q):
        at_y = (y + jnp.where(q == 1, 3, jnp.where(q == 2, 1, jnp.where(q == 3, 2, 0)))) % Y_N
        panel = q < 4
        found = []
        for u, k in enumerate(order):
            start = jnp.where(panel, place(k, at_y * ZH_N), (q + 1) * b + min(u, 1) * h)
            there = jnp.logical_or(panel, u < 2) if u < 2 else jnp.logical_and(panel, at_y < Y_N // 2)
            found.append((there, pl.ds(pl.multiple_of(start, h), h)))
        return found

    def tree_copy(source, at, q, u, child, device):
        return remote(source.at[at], pack_r.at[at], tree_send.at[child, q, u], tree_recv.at[q, u], device)

    def hand_down(source, q):
        for u, (there, at) in enumerate(units(q)):
            for child, (wanted, device) in enumerate(children(q)):

                @pl.when(jnp.logical_and(wanted, there))
                def _():
                    tree_copy(source, at, q, u, child, device).start()

    def root_gives(q):
        @pl.when(is_root)
        def _():
            hand_down(pack_l, jnp.int32(q))

    def poll(p):
        q = p - depth

        @pl.when(jnp.logical_and(depth > 0, jnp.logical_and(q >= 0, q < CHUNKS)))
        def _():
            now = jnp.clip(q, 0, CHUNKS - 1)
            for u, (there, at) in enumerate(units(now)):

                @pl.when(there)
                def _():
                    tree_copy(pack_r, at, now, u, 0, core_dev).wait_recv()

            hand_down(pack_r, now)

    def y_copy(side, k, at_y):
        block = rows(k, col_of(at_y, 0), 0, 4 * piece)
        return remote(block, block, y_send.at[side, k], y_recv.at[side, k], y_dev[side])

    def pass_copy(side, k, at_y):
        block = rows(k, col_of(at_y, 0), side * 2 * piece, 2 * piece)
        return remote(block, block, f_send.at[side, k], f_recv.at[side, k], y_dev[side])

    for k in order:
        own_copy(k).wait()
        for d in range(3):
            z_copy(d, k, col_of(y, (zh + ZH_N - 1 - d) % ZH_N)).wait_recv()
        for side in range(2):
            y_copy(side, k, y).start()
    root_gives(0)

    tile_in.wait()

    @pl.when(active)
    def _():
        @pl.loop(0, 8)
        def _(i):
            at = pl.ds(pl.multiple_of(i * h, h), h)
            high[at, :], low[at, :] = split(tile[at, :])

    sources = (y_dn, y_up)
    for k in order:
        for side in range(2):
            y_copy(side, k, sources[side]).wait_recv()
            pass_copy(side, k, sources[side]).start()
    root_gives(1)
    root_gives(2)
    poll(1)
    far = (y + 2) % Y_N
    for k in order:
        for side in range(2):
            pass_copy(side, k, far).wait_recv()
    root_gives(3)

    def bottom_copy():
        return remote(pack_l.at[8 * b : 9 * b], pack_l.at[5 * b : 6 * b], n_send.at[0], n_recv.at[0], dn_dev)

    def factor_copy():
        return remote(
            pack_l.at[7 * b : 7 * b + h], pack_l.at[7 * b + h : 8 * b], n_send.at[1], n_recv.at[1], dn_dev
        )

    @pl.when(has_dn)
    def _():
        bottom_copy().start()

    poll(2)
    plan_in.wait()

    f_row = {0: 6 * b, 2: 6 * b + h, 1: 7 * b, 3: 7 * b + h}

    def keep_f(pack, slot, turned):
        value = pack[f_row[slot] : f_row[slot] + h, :]
        f_h[slot], f_l[slot] = split(value.T if turned else value)

    @pl.when(active)
    def _():
        at_row = lax.broadcasted_iota(jnp.int32, (h, h), 0)
        at_col = lax.broadcasted_iota(jnp.int32, (h, h), 1)
        eye = jnp.where(at_row == at_col, 1.0, 0.0).astype(F32)
        panels = [[pack_l[0 : 2 * b, :]], [pack_l[4 * b : 5 * b, :], pack_l[8 * b : 9 * b, :]], [pack_l[2 * b : 4 * b, :]]]
        powers, results, scales = [], [], []
        for parts in panels:
            gram = sum(exact_dot(part.T, part) for part in parts)
            upper = jnp.where(at_row < at_col, gram, jnp.where(at_row == at_col, gram * 0.5, 0.0))
            diag = jnp.where(at_row == at_col, upper, 0.0)
            power = eye - upper * (1.0 / jnp.sum(diag, axis=1, keepdims=True))
            powers.append(power)
            results.append(eye + power)
            scales.append(1.0 / jnp.sum(diag, axis=0, keepdims=True))
        span = 2
        while span < h:
            powers = [exact_dot(power, power) for power in powers]
            results = [result + exact_dot(result, power) for result, power in zip(results, powers)]
            span = span * 2
        live = [
            plan_ref[0, r] > 0,
            jnp.logical_and(plan_ref[1, r] > 0, r < rows_n - 1),
            plan_ref[2, r] > 0,
        ]
        for k in range(3):
            factor = jnp.where(live[k], results[k] * scales[k], 0.0)
            pack_l[f_row[k] : f_row[k] + h, :] = factor
            f_h[k], f_l[k] = split(factor.T)

    @pl.when(has_dn)
    def _():
        factor_copy().start()

    @pl.when(has_up)
    def _():
        bottom_copy().wait_recv()

    root_gives(4)
    root_gives(5)
    poll(3)

    def operators(pack):
        pairs = [
            jnp.concatenate([pack[0:b, :], pack[5 * b : 6 * b, :]], axis=1),
            jnp.concatenate([pack[b : 2 * b, :], pack[2 * b : 3 * b, :]], axis=1),
        ]
        thin = [pack[3 * b : 4 * b, :], pack[4 * b : 5 * b, :]]
        for at in range(2):
            pair_h[at], pair_l[at] = split(pairs[at])
            thin_h[at], thin_l[at] = split(thin[at])
        first = exact_dot(pack[5 * b : 6 * b, :].T, pack[0:b, :])
        second = exact_dot(pack[2 * b : 3 * b, :].T, pack[b : 2 * b, :])
        cc_h[...], cc_l[...] = split(jnp.concatenate([first, second], axis=0))
        return pairs, thin

    def pair(at):
        return pair_h[at], pair_l[at]

    def thinner(at):
        return thin_h[at], thin_l[at]

    def turned(at):
        return turn_h[at], turn_l[at]

    def tthin(at):
        return tthin_h[at], tthin_l[at]

    def f_of(k):
        return f_h[k], f_l[k]

    def c_of():
        return cc_h[...], cc_l[...]

    band = [slice(i * b, (i + 1) * b) for i in range(4)]

    def band_of(i):
        return high[band[i], :], low[band[i], :]

    def lower_band(i, value):
        value = tile[band[i], :] - value
        tile[band[i], :] = value
        high[band[i], :], low[band[i], :] = split(value)

    def t_copy():
        return remote(t_own, from_above, row_send.at[0], row_recv.at[0], dn_dev)

    def p_copy():
        return remote(p_own, from_below, row_send.at[1], row_recv.at[1], up_dev)

    @pl.when(active)
    def _():
        pairs, thin = operators(pack_l)
        for at in range(2):
            turn_h[at], turn_l[at] = split(pairs[at].T)
            tthin_h[at], tthin_l[at] = split(thin[at].T)
        t_own[...] = dot3(tthin(1), band_of(3))

    @pl.when(has_dn)
    def _():
        t_copy().start()

    poll(4)

    @pl.when(active)
    def _():
        x0 = dot3(turned(0), band_of(0))
        x1 = dot3(turned(1), band_of(1))
        p_own[...] = x0[h:]
        t0_h[...], t0_l[...] = split(x0[:h] + x1[:h])
        t2_own[...] = x1[h:] + dot3(tthin(0), band_of(2))
        u0 = split(dot3(f_of(0), (t0_h[...], t0_l[...])))
        t0_h[...], t0_l[...] = u0
        shift = dot3(c_of(), u0)
        p_own[...] = p_own[...] - shift[:h]
        u2_h[...], u2_l[...] = split(dot3(f_of(2), split(t2_own[...] - shift[h:])))

    @pl.when(has_up)
    def _():
        p_copy().start()
        factor_copy().wait_recv()

    root_gives(6)
    poll(5)
    poll(6)

    @pl.when(active)
    def _():
        u0, u2 = (t0_h[...], t0_l[...]), (u2_h[...], u2_l[...])
        lower_band(1, dot3(pair(1), join(u0, u2, 0)))
        lower_band(2, dot3(thinner(0), u2))
        keep_f(pack_l, 3, True)

    @pl.when(is_root)
    def _():
        pack_r[...] = pack_l[0 : 8 * b, :]

    poll(7)

    @pl.when(has_dn)
    def _():
        p_copy().wait_recv()

    @pl.when(has_up)
    def _():
        t_copy().wait_recv()

    @pl.when(active)
    def _():
        u1 = split(dot3(f_of(1), split(t_own[...] + from_below[...])))
        u1p = split(dot3(f_of(3), split(from_above[...] + p_own[...])))
        lower_band(0, dot3(pair(0), join((t0_h[...], t0_l[...]), u1p, 0)))
        lower_band(3, dot3(thinner(1), u1))

    poll(8)
    poll(9)

    def st_copy(i):
        return remote(st_own.at[i], from_left.at[i], rt_send.at[i], rt_recv.at[i], rt_dev)

    def sb_copy(i):
        return remote(sb_own.at[i], from_right.at[i], lf_send.at[i], lf_recv.at[i], lf_dev)

    def out_copy(i):
        at = pl.ds(pl.multiple_of(i * (2 * b), 2 * b), 2 * b)
        return pltpu.make_async_copy(tile.at[at], out_ref.at[at], out_sem.at[i])

    def cut(at, j):
        return high[at, band[j]], low[at, band[j]]

    @pl.when(active)
    def _():
        operators(pack_r)
        keep_f(pack_r, 0, False)
        keep_f(pack_r, 2, False)

    halves = [slice(i * 2 * b, (i + 1) * 2 * b) for i in range(2)]
    for i, at in enumerate(halves):

        @pl.when(active)
        def _():
            st_own[i] = dot3(cut(at, 3), thinner(1))
            x0 = dot3(cut(at, 0), pair(0))
            x1 = dot3(cut(at, 1), pair(1))
            y0 = split(dot3(split(x0[:, :h] + x1[:, :h]), f_of(0)))
            y0_h[i], y0_l[i] = y0
            shift = dot3(y0, c_of(), turned=True)
            sb_own[i] = x0[:, h:] - shift[:, :h]
            x2 = dot3(cut(at, 2), thinner(0))
            y2_of = split(dot3(split(x1[:, h:] + x2 - shift[:, h:]), f_of(2)))

            @pl.when(has_rt)
            def _():
                st_copy(i).start()

            @pl.when(has_lf)
            def _():
                sb_copy(i).start()

            tile[at, band[1]] = tile[at, band[1]] - dot3(join(y0, y2_of, 1), pair(1), turned=True)
            tile[at, band[2]] = tile[at, band[2]] - dot3(y2_of, thinner(0), turned=True)

    poll(10)

    @pl.when(active)
    def _():
        keep_f(pack_r, 1, False)
        keep_f(pack_r, 3, False)

    for i, at in enumerate(halves):

        @pl.when(has_rt)
        def _():
            sb_copy(i).wait_recv()

        @pl.when(has_lf)
        def _():
            st_copy(i).wait_recv()

        @pl.when(active)
        def _():
            y1 = split(dot3(split(st_own[i] + from_right[i]), f_of(1)))
            y1p = split(dot3(split(from_left[i] + sb_own[i]), f_of(3)))
            tile[at, band[0]] = tile[at, band[0]] - dot3(join((y0_h[i], y0_l[i]), y1p, 1), pair(0), turned=True)
            tile[at, band[3]] = tile[at, band[3]] - dot3(y1, thinner(1), turned=True)

        out_copy(i).start()

    for k in range(3):
        for d in range(3):
            z_copy(d, k, c).wait_send()
        for side in range(2):
            y_copy(side, k, y).wait_send()
            pass_copy(side, k, sources[side]).wait_send()

    @pl.when(has_dn)
    def _():
        bottom_copy().wait_send()
        factor_copy().wait_send()
        t_copy().wait_send()

    @pl.when(has_up)
    def _():
        p_copy().wait_send()

    @pl.loop(0, CHUNKS)
    def _(q):
        for u, (there, at) in enumerate(units(q)):
            for child, (wanted, device) in enumerate(children(q)):

                @pl.when(jnp.logical_and(wanted, there))
                def _():
                    tree_copy(pack_r, at, q, u, child, device).wait_send()

    for i in range(2):

        @pl.when(has_rt)
        def _():
            st_copy(i).wait_send()

        @pl.when(has_lf)
        def _():
            sb_copy(i).wait_send()

        out_copy(i).wait()


def solution(mesh):
    rows_n, cols_n = mesh.shape["row"], mesh.shape["col"]

    def on_device(matrix_tiles, panels, plan):
        size, refl = matrix_tiles.shape[-1], panels.shape[-1]
        b, h = size // 4, refl
        piece = panels.shape[3]
        vmem, dma = pltpu.VMEM, pltpu.SemaphoreType.DMA
        scratch = [
            pltpu.SMEM(plan.shape, jnp.int32), vmem((9 * b, h), F32), vmem((8 * b, h), F32), vmem((size, size), F32),
            vmem((size, size), BF16), vmem((size, size), BF16),
            vmem((2, b, b), BF16), vmem((2, b, b), BF16), vmem((2, b, h), BF16), vmem((2, b, h), BF16),
            vmem((2, b, b), BF16), vmem((2, b, b), BF16), vmem((2, h, b), BF16), vmem((2, h, b), BF16),
            vmem((4, h, h), BF16), vmem((4, h, h), BF16), vmem((b, h), BF16), vmem((b, h), BF16),
            vmem((h, size), BF16), vmem((h, size), BF16), vmem((h, size), F32), vmem((h, size), BF16), vmem((h, size), BF16),
            vmem((h, size), F32), vmem((h, size), F32), vmem((h, size), F32), vmem((h, size), F32),
            vmem((2, 2 * b, h), F32), vmem((2, 2 * b, h), F32), vmem((2, 2 * b, h), F32), vmem((2, 2 * b, h), F32),
            vmem((2, 2 * b, h), BF16), vmem((2, 2 * b, h), BF16),
            dma((2,)), dma((3,)), dma((2,)),
            dma((3, 3)), dma((3, 3)), dma((2, 3)), dma((2, 3)), dma((2, 3)), dma((2, 3)), dma((2,)), dma((2,)),
            dma((4, CHUNKS, 3)), dma((CHUNKS, 3)), dma((2,)), dma((2,)), dma((2,)), dma((2,)), dma((2,)), dma((2,)),
        ]
        result = pl.pallas_call(
            functools.partial(kernel, rows_n, cols_n, b),
            out_shape=jax.ShapeDtypeStruct((size, size), F32),
            in_specs=[pl.BlockSpec(memory_space=pl.ANY)] * 3,
            out_specs=pl.BlockSpec(memory_space=pl.ANY),
            scratch_shapes=scratch,
            compiler_params=pltpu.CompilerParams(
                collective_id=0, has_side_effects=True, vmem_limit_bytes=60 * 1024 * 1024
            ),
        )(matrix_tiles.reshape(size, size), panels.reshape(3, piece, refl), plan)
        return result.reshape(matrix_tiles.shape)

    placed = (P(None, "row", None, "col", None, None), P(None, None, "row", "col", None), P())
    return jax.shard_map(
        on_device,
        mesh=mesh,
        in_specs=placed,
        out_specs=P(None, "row", None, "col", None, None),
        check_vma=False,
    )
```

```python
import functools

import jax
import jax.numpy as jnp
from jax import lax
from jax.experimental import pallas as pl
from jax.experimental.pallas import tpu as pltpu
from jax.sharding import PartitionSpec as P

MESH = pl.DeviceIdType.MESH
F32 = jnp.float32
BF16 = jnp.bfloat16

X_N, CORE_N, Y_N, ZH_N = 4, 2, 4, 4
CHUNKS = 7


def split(value):
    high = value.astype(BF16)
    low = (value - high.astype(F32)).astype(BF16)
    return high, low


def dot3(left, right, turned=False):
    side = 1 if turned else 0
    a = jnp.concatenate([left[0], left[0], left[1]], axis=1)
    z = jnp.concatenate([right[0], right[1], right[0]], axis=side)
    return lax.dot_general(a, z, (((1,), (side,)), ((), ())), preferred_element_type=F32)


def join(first, second, axis):
    return tuple(jnp.concatenate([a, z], axis=axis) for a, z in zip(first, second))


def exact_dot(left, right):
    return jnp.dot(left, right, precision=lax.Precision.HIGHEST, preferred_element_type=F32)


def kernel(
    rows_n, cols_n, b, h_ref, panel_ref, plan_hbm, out_ref,
    plan_ref, v_l, x_l, v_r, x_r, tile, high, low, pair_h, pair_l, thin_h, thin_l, turn_h, turn_l, tthin_h, tthin_l,
    f_h, f_l, cc_h, cc_l, t0_h, t0_l, t2_own, u2_h, u2_l, t_own, p_own, from_below, from_above,
    st_own, sb_own, from_right, from_left, y0_h, y0_l, y2_own,
    in_sem, out_sem, g_send, g_recv, y_send, y_recv, f_send, f_recv, n_send, n_recv,
    tree_send, tree_recv, row_send, row_recv, rt_send, rt_recv, lf_send, lf_recv,
):
    h = b // 2
    piece = 2 * b // cols_n
    r = lax.axis_index("row")
    c = lax.axis_index("col")
    zl, x, core = r // (X_N * CORE_N), (r // CORE_N) % X_N, r % CORE_N
    y, zh = c // ZH_N, c % ZH_N

    def row_of(zl, x, core):
        return zl * (X_N * CORE_N) + x * CORE_N + core

    def col_of(y, zh):
        return y * ZH_N + zh

    active = r <= c + 1
    has_up = jnp.logical_and(active, r > 0)
    has_dn = jnp.logical_and(r < rows_n - 1, r <= c)
    has_rt = jnp.logical_and(active, c < cols_n - 1)
    has_lf = jnp.logical_and(r <= c, c > 0)

    up_dev, dn_dev = (r - 1, c), (r + 1, c)
    rt_dev, lf_dev = (r, c + 1), (r, c - 1)
    zh_dev = [(r, col_of(y, (zh + d) % ZH_N)) for d in (1, 2, 3)]
    y_up, y_dn = (y + 1) % Y_N, (y + Y_N - 1) % Y_N
    y_dev = [(r, col_of(y_up, zh)), (r, col_of(y_dn, zh))]
    core_dev = (row_of(zl, x, 1 - core), c)
    z_dev = (row_of(1 - zl, x, core), c)
    xp_dev = (row_of(zl, (x + 1) % X_N, core), c)
    xm_dev = (row_of(zl, (x + X_N - 1) % X_N, core), c)

    def remote(src, dst, send, recv, device):
        return pltpu.make_async_remote_copy(
            src_ref=src, dst_ref=dst, send_sem=send, recv_sem=recv, device_id=device, device_id_type=MESH
        )

    tile_in = pltpu.make_async_copy(h_ref, tile, in_sem.at[0])
    plan_in = pltpu.make_async_copy(plan_hbm, plan_ref, in_sem.at[1])
    plan_in.start()
    tile_in.start()

    barrier = pltpu.get_barrier_semaphore()
    around = [((r + step) % rows_n, c) for step in (1, rows_n - 1)] + [(r, (c + step) % cols_n) for step in (1, cols_n - 1)]
    peers = zh_dev + y_dev + [core_dev, z_dev, xp_dev, xm_dev] + around
    for device in peers:
        pl.semaphore_signal(barrier, inc=1, device_id=device, device_id_type=MESH)
    pl.semaphore_wait(barrier, len(peers))

    def z_copy(d, at_zh):
        at = v_l.at[y, :, pl.ds(pl.multiple_of(at_zh * piece, piece), piece)]
        return remote(panel_ref, at, g_send.at[d], g_recv.at[d], zh_dev[d])

    own_copy = pltpu.make_async_copy(panel_ref, v_l.at[y, :, pl.ds(pl.multiple_of(zh * piece, piece), piece)], in_sem.at[2])
    for d in range(3):
        z_copy(d, zh).start()
    own_copy.start()

    @pl.when(jnp.logical_not(has_dn))
    def _():
        from_below[...] = jnp.zeros_like(from_below)

    @pl.when(jnp.logical_not(has_up))
    def _():
        from_above[...] = jnp.zeros_like(from_above)
        x_l[0:2] = jnp.zeros((2, h, h), F32)
        x_l[5] = jnp.zeros((h, h), F32)

    @pl.when(jnp.logical_not(has_rt))
    def _():
        from_right[...] = jnp.zeros_like(from_right)

    @pl.when(jnp.logical_not(has_lf))
    def _():
        from_left[...] = jnp.zeros_like(from_left)

    root_zl, root_x, root_core = c // (X_N * CORE_N), (c // CORE_N) % X_N, c % CORE_N
    dx = (x + X_N - root_x) % X_N
    dz = jnp.where(zl == root_zl, 0, 1)
    dc = jnp.where(core == root_core, 0, 1)
    depth = dz + dc + jnp.where(dx == 0, 0, jnp.where(dx == 2, 2, 1))
    own = dc == 0
    is_root = r == c

    def children(q):
        even = q % 2 == 0
        odd = q % 2 == 1
        return [
            (jnp.logical_and(own, jnp.logical_or(dx == 0, jnp.logical_and(dx == 1, even))), xp_dev),
            (jnp.logical_and(own, jnp.logical_or(dx == 0, jnp.logical_and(dx == 3, odd))), xm_dev),
            (is_root, z_dev),
            (own, core_dev),
        ]

    def tree_copy(v_from, x_from, panel, q, child, device):
        send, recv = tree_send.at[child, q], tree_recv.at[q]
        if panel:
            at_y = (y + jnp.where(q == 1, 3, jnp.where(q == 2, 1, jnp.where(q == 3, 2, 0)))) % Y_N
            return remote(v_from.at[at_y], v_r.at[at_y], send, recv, device)
        at = pl.ds(2 * (q - 4), 2)
        return remote(x_from.at[at], x_r.at[at], send, recv, device)

    def hand_down(v_from, x_from, panel, q):
        for child, (wanted, device) in enumerate(children(q)):

            @pl.when(wanted)
            def _():
                tree_copy(v_from, x_from, panel, q, child, device).start()

    def root_gives(q):
        @pl.when(is_root)
        def _():
            hand_down(v_l, x_l, q < 4, jnp.int32(q))

    def poll(p):
        q = p - depth
        for panel, least, top in ((True, 0, 3), (False, 4, CHUNKS - 1)):
            if p >= least + 1:

                @pl.when(jnp.logical_and(depth > 0, jnp.logical_and(q >= least, q <= top)))
                def _():
                    now = jnp.clip(q, least, top)
                    tree_copy(v_r, x_r, panel, now, 0, core_dev).wait_recv()
                    hand_down(v_r, x_r, panel, now)

    def y_copy(side, at_y):
        block = v_l.at[at_y]
        return remote(block, block, y_send.at[side], y_recv.at[side], y_dev[side])

    def pass_copy(side, at_y):
        block = v_l.at[at_y, :, side * 2 * piece : (side + 1) * 2 * piece]
        return remote(block, block, f_send.at[side], f_recv.at[side], y_dev[side])

    own_copy.wait()
    for d in range(3):
        z_copy(d, (zh + ZH_N - 1 - d) % ZH_N).wait_recv()
    for side in range(2):
        y_copy(side, y).start()
    root_gives(0)

    tile_in.wait()

    @pl.when(active)
    def _():
        @pl.loop(0, 8)
        def _(i):
            at = pl.ds(pl.multiple_of(i * h, h), h)
            high[at, :], low[at, :] = split(tile[at, :])

    sources = (y_dn, y_up)
    for side in range(2):
        y_copy(side, sources[side]).wait_recv()
        pass_copy(side, sources[side]).start()
    root_gives(1)
    root_gives(2)
    poll(1)
    far = (y + 2) % Y_N
    for side in range(2):
        pass_copy(side, far).wait_recv()
    root_gives(3)

    def bottom_copy():
        return remote(v_l.at[2:4, 1], x_l.at[0:2], n_send.at[0], n_recv.at[0], dn_dev)

    def factor_copy():
        return remote(x_l.at[4], x_l.at[5], n_send.at[1], n_recv.at[1], dn_dev)

    @pl.when(has_dn)
    def _():
        bottom_copy().start()

    poll(2)
    plan_in.wait()

    f_at = {0: 2, 2: 3, 1: 4, 3: 5}

    @pl.when(active)
    def _():
        at_row = lax.broadcasted_iota(jnp.int32, (h, h), 0)
        at_col = lax.broadcasted_iota(jnp.int32, (h, h), 1)
        eye = jnp.where(at_row == at_col, 1.0, 0.0).astype(F32)
        powers, results, scales = [], [], []
        for k in range(3):
            panel = jnp.concatenate([v_l[at, k] for at in range(4)], axis=0)
            gram = exact_dot(panel.T, panel)
            upper = jnp.where(at_row < at_col, gram, jnp.where(at_row == at_col, gram * 0.5, 0.0))
            diag = jnp.where(at_row == at_col, upper, 0.0)
            power = eye - upper * (1.0 / jnp.sum(diag, axis=1, keepdims=True))
            powers.append(power)
            results.append(eye + power)
            scales.append(1.0 / jnp.sum(diag, axis=0, keepdims=True))
        span = 2
        while span < h:
            powers = [exact_dot(power, power) for power in powers]
            results = [result + exact_dot(result, power) for result, power in zip(results, powers)]
            span = span * 2
        live = [
            plan_ref[0, r] > 0,
            jnp.logical_and(plan_ref[1, r] > 0, r < rows_n - 1),
            plan_ref[2, r] > 0,
        ]
        for k in range(3):
            factor = jnp.where(live[k], results[k] * scales[k], 0.0)
            x_l[f_at[k]] = factor
            f_h[k], f_l[k] = split(factor.T)

    @pl.when(has_dn)
    def _():
        factor_copy().start()

    @pl.when(has_up)
    def _():
        bottom_copy().wait_recv()

    root_gives(4)
    root_gives(5)
    poll(3)

    def operators(side, v, x):
        def top(k):
            return jnp.concatenate([v[0, k], v[1, k]], axis=0)

        def bottom(k):
            return jnp.concatenate([v[2, k], v[3, k]], axis=0)

        before = jnp.concatenate([x[0], x[1]], axis=0)
        pairs = [jnp.concatenate([top(0), before], axis=1), jnp.concatenate([bottom(0), top(2)], axis=1)]
        thin = [bottom(2), top(1)]
        for at in range(2):
            pair_h[2 * side + at], pair_l[2 * side + at] = split(pairs[at])
            thin_h[2 * side + at], thin_l[2 * side + at] = split(thin[at])
        first = exact_dot(before.T, top(0))
        second = exact_dot(top(2).T, bottom(0))
        cc_h[...], cc_l[...] = split(jnp.concatenate([first, second], axis=0))
        return pairs, thin

    def pair(at):
        return pair_h[at], pair_l[at]

    def thinner(at):
        return thin_h[at], thin_l[at]

    def turned(at):
        return turn_h[at], turn_l[at]

    def tthin(at):
        return tthin_h[at], tthin_l[at]

    def f_of(k):
        return f_h[k], f_l[k]

    def c_of():
        return cc_h[...], cc_l[...]

    band = [slice(i * b, (i + 1) * b) for i in range(4)]

    def band_of(i):
        return high[band[i], :], low[band[i], :]

    def lower_band(i, value):
        value = tile[band[i], :] - value
        tile[band[i], :] = value
        high[band[i], :], low[band[i], :] = split(value)

    def t_copy():
        return remote(t_own, from_above, row_send.at[0], row_recv.at[0], dn_dev)

    def p_copy():
        return remote(p_own, from_below, row_send.at[1], row_recv.at[1], up_dev)

    @pl.when(active)
    def _():
        pairs, thin = operators(0, v_l, x_l)
        for at in range(2):
            turn_h[at], turn_l[at] = split(pairs[at].T)
            tthin_h[at], tthin_l[at] = split(thin[at].T)
        t_own[...] = dot3(tthin(1), band_of(3))

    @pl.when(has_dn)
    def _():
        t_copy().start()

    poll(4)

    @pl.when(active)
    def _():
        x0 = dot3(turned(0), band_of(0))
        x1 = dot3(turned(1), band_of(1))
        p_own[...] = x0[h:]
        t0_h[...], t0_l[...] = split(x0[:h] + x1[:h])
        t2_own[...] = x1[h:] + dot3(tthin(0), band_of(2))
        u0 = split(dot3(f_of(0), (t0_h[...], t0_l[...])))
        t0_h[...], t0_l[...] = u0
        shift = dot3(c_of(), u0)
        p_own[...] = p_own[...] - shift[:h]
        u2_h[...], u2_l[...] = split(dot3(f_of(2), split(t2_own[...] - shift[h:])))

    @pl.when(has_up)
    def _():
        p_copy().start()
        factor_copy().wait_recv()

    root_gives(6)
    poll(5)
    poll(6)

    @pl.when(active)
    def _():
        u0, u2 = (t0_h[...], t0_l[...]), (u2_h[...], u2_l[...])
        lower_band(1, dot3(pair(1), join(u0, u2, 0)))
        lower_band(2, dot3(thinner(0), u2))
        f_h[3], f_l[3] = split(x_l[5].T)

    @pl.when(is_root)
    def _():
        v_r[...] = v_l[...]
        x_r[...] = x_l[...]

    poll(7)

    poll(8)
    poll(9)

    def st_copy(i):
        return remote(st_own.at[i], from_left.at[i], rt_send.at[i], rt_recv.at[i], rt_dev)

    def sb_copy(i):
        return remote(sb_own.at[i], from_right.at[i], lf_send.at[i], lf_recv.at[i], lf_dev)

    parts = [(slice(b, 3 * b),), (slice(0, b), slice(3 * b, 4 * b))]

    def out_copies(i):
        return [
            pltpu.make_async_copy(tile.at[at], out_ref.at[at], out_sem.at[i + n]) for n, at in enumerate(parts[i])
        ]

    def cut(i, j):
        return tuple(jnp.concatenate([ref[at, band[j]] for at in parts[i]], axis=0) for ref in (high, low))

    def lower_cols(i, j, value):
        done = 0
        for at in parts[i]:
            count = at.stop - at.start
            tile[at, band[j]] = tile[at, band[j]] - value[done : done + count]
            done = done + count

    def right_start(i):
        @pl.when(active)
        def _():
            st_own[i] = dot3(cut(i, 3), thinner(3))

        @pl.when(has_rt)
        def _():
            st_copy(i).start()

        @pl.when(active)
        def _():
            x0 = dot3(cut(i, 0), pair(2))
            x1 = dot3(cut(i, 1), pair(3))
            y0 = split(dot3(split(x0[:, :h] + x1[:, :h]), f_of(4)))
            y0_h[i], y0_l[i] = y0
            shift = dot3(y0, c_of(), turned=True)
            sb_own[i] = x0[:, h:] - shift[:, :h]
            y2_own[...] = x1[:, h:] - shift[:, h:]

        @pl.when(has_lf)
        def _():
            sb_copy(i).start()

    def right_middle(i):
        @pl.when(active)
        def _():
            y2_of = split(dot3(split(y2_own[...] + dot3(cut(i, 2), thinner(2))), f_of(6)))
            lower_cols(i, 1, dot3(join((y0_h[i], y0_l[i]), y2_of, 1), pair(3), turned=True))
            lower_cols(i, 2, dot3(y2_of, thinner(2), turned=True))

    def right_end(i):
        @pl.when(has_rt)
        def _():
            sb_copy(i).wait_recv()

        @pl.when(has_lf)
        def _():
            st_copy(i).wait_recv()

        @pl.when(active)
        def _():
            y1 = split(dot3(split(st_own[i] + from_right[i]), f_of(5)))
            y1p = split(dot3(split(from_left[i] + sb_own[i]), f_of(7)))
            lower_cols(i, 0, dot3(join((y0_h[i], y0_l[i]), y1p, 1), pair(2), turned=True))
            lower_cols(i, 3, dot3(y1, thinner(3), turned=True))

        for copy in out_copies(i):
            copy.start()

    @pl.when(active)
    def _():
        operators(1, v_r, x_r)
        f_h[4], f_l[4] = split(x_r[2])
        f_h[6], f_l[6] = split(x_r[3])

    right_start(0)

    @pl.when(has_dn)
    def _():
        p_copy().wait_recv()

    @pl.when(has_up)
    def _():
        t_copy().wait_recv()

    @pl.when(active)
    def _():
        u1 = split(dot3(f_of(1), split(t_own[...] + from_below[...])))
        u1p = split(dot3(f_of(3), split(from_above[...] + p_own[...])))
        lower_band(0, dot3(pair(0), join((t0_h[...], t0_l[...]), u1p, 0)))
        lower_band(3, dot3(thinner(1), u1))

    right_middle(0)
    right_start(1)
    right_middle(1)
    poll(10)

    @pl.when(active)
    def _():
        f_h[5], f_l[5] = split(x_r[4])
        f_h[7], f_l[7] = split(x_r[5])

    right_end(0)
    right_end(1)

    for d in range(3):
        z_copy(d, zh).wait_send()
    for side in range(2):
        y_copy(side, y).wait_send()
        pass_copy(side, sources[side]).wait_send()

    @pl.when(has_dn)
    def _():
        bottom_copy().wait_send()
        factor_copy().wait_send()
        t_copy().wait_send()

    @pl.when(has_up)
    def _():
        p_copy().wait_send()

    for panel, least, top in ((True, 0, 4), (False, 4, CHUNKS)):

        @pl.loop(least, top)
        def _(q):
            for child, (wanted, device) in enumerate(children(q)):

                @pl.when(wanted)
                def _():
                    tree_copy(v_r, x_r, panel, q, child, device).wait_send()

    for i in range(2):

        @pl.when(has_rt)
        def _():
            st_copy(i).wait_send()

        @pl.when(has_lf)
        def _():
            sb_copy(i).wait_send()

        for copy in out_copies(i):
            copy.wait()


def solution(mesh):
    rows_n, cols_n = mesh.shape["row"], mesh.shape["col"]

    def on_device(matrix_tiles, panels, plan):
        size, refl = matrix_tiles.shape[-1], panels.shape[-1]
        b, h = size // 4, refl
        piece = panels.shape[3]
        vmem, dma = pltpu.VMEM, pltpu.SemaphoreType.DMA
        scratch = [
            pltpu.SMEM(plan.shape, jnp.int32),
            vmem((4, 3, h, h), F32), vmem((6, h, h), F32), vmem((4, 3, h, h), F32), vmem((6, h, h), F32),
            vmem((size, size), F32), vmem((size, size), BF16), vmem((size, size), BF16),
            vmem((4, b, b), BF16), vmem((4, b, b), BF16), vmem((4, b, h), BF16), vmem((4, b, h), BF16),
            vmem((2, b, b), BF16), vmem((2, b, b), BF16), vmem((2, h, b), BF16), vmem((2, h, b), BF16),
            vmem((8, h, h), BF16), vmem((8, h, h), BF16), vmem((b, h), BF16), vmem((b, h), BF16),
            vmem((h, size), BF16), vmem((h, size), BF16), vmem((h, size), F32), vmem((h, size), BF16), vmem((h, size), BF16),
            vmem((h, size), F32), vmem((h, size), F32), vmem((h, size), F32), vmem((h, size), F32),
            vmem((2, 2 * b, h), F32), vmem((2, 2 * b, h), F32), vmem((2, 2 * b, h), F32), vmem((2, 2 * b, h), F32),
            vmem((2, 2 * b, h), BF16), vmem((2, 2 * b, h), BF16), vmem((2 * b, h), F32),
            dma((3,)), dma((3,)),
            dma((3,)), dma((3,)), dma((2,)), dma((2,)), dma((2,)), dma((2,)), dma((2,)), dma((2,)),
            dma((4, CHUNKS)), dma((CHUNKS,)), dma((2,)), dma((2,)), dma((2,)), dma((2,)), dma((2,)), dma((2,)),
        ]
        result = pl.pallas_call(
            functools.partial(kernel, rows_n, cols_n, b),
            out_shape=jax.ShapeDtypeStruct((size, size), F32),
            in_specs=[pl.BlockSpec(memory_space=pltpu.HBM)] * 3,
            out_specs=pl.BlockSpec(memory_space=pl.ANY),
            scratch_shapes=scratch,
            compiler_params=pltpu.CompilerParams(
                collective_id=0, has_side_effects=True, vmem_limit_bytes=48 * 1024 * 1024
            ),
        )(matrix_tiles.reshape(size, size), panels.reshape(3, piece, refl), plan)
        return result.reshape(matrix_tiles.shape)

    placed = (P(None, "row", None, "col", None, None), P(None, None, "row", "col", None), P())
    return jax.shard_map(
        on_device,
        mesh=mesh,
        in_specs=placed,
        out_specs=P(None, "row", None, "col", None, None),
        check_vma=False,
    )
```

```python
import functools

import jax
import jax.numpy as jnp
from jax import lax
from jax.experimental import pallas as pl
from jax.experimental.pallas import tpu as pltpu
from jax.sharding import PartitionSpec as P

MESH = pl.DeviceIdType.MESH
F32 = jnp.float32
BF16 = jnp.bfloat16

X_N, CORE_N, Y_N, ZH_N = 4, 2, 4, 4


def split(value):
    high = value.astype(BF16)
    low = (value - high.astype(F32)).astype(BF16)
    return high, low


def dot3(left, right, turned=False):
    side = 1 if turned else 0
    a = jnp.concatenate([left[0], left[0], left[1]], axis=1)
    z = jnp.concatenate([right[0], right[1], right[0]], axis=side)
    return lax.dot_general(a, z, (((1,), (side,)), ((), ())), preferred_element_type=F32)


def join(first, second, axis):
    return tuple(jnp.concatenate([a, z], axis=axis) for a, z in zip(first, second))


def exact_dot(left, right):
    return jnp.dot(left, right, precision=lax.Precision.HIGHEST, preferred_element_type=F32)


def kernel(
    rows_n, cols_n, b, h_ref, panel_ref, plan_hbm, out_ref,
    plan_ref, v_l, x_l, v_r, x_r, tile, high, low, pair_h, pair_l, thin_h, thin_l, turn_h, turn_l, tthin_h, tthin_l,
    f_h, f_l, cc_h, cc_l, t0_h, t0_l, t2_own, u2_h, u2_l, t_own, p_own, from_below, from_above,
    st_own, sb_own, from_right, from_left, y0_h, y0_l, y2_own,
    in_sem, out_sem, g_send, g_recv, y_send, y_recv, f_send, f_recv, n_send, n_recv,
    c_send, c_recv, d_send, d_recv, k_send, k_recv, m_send, m_recv, row_send, row_recv, rt_send, rt_recv, lf_send, lf_recv,
):
    h = b // 2
    piece = 2 * b // cols_n
    r = lax.axis_index("row")
    c = lax.axis_index("col")
    zl, x, core = r // (X_N * CORE_N), (r // CORE_N) % X_N, r % CORE_N
    y, zh = c // ZH_N, c % ZH_N

    def row_of(zl, x, core):
        return zl * (X_N * CORE_N) + x * CORE_N + core

    def col_of(y, zh):
        return y * ZH_N + zh

    active = r <= c + 1
    has_up = jnp.logical_and(active, r > 0)
    has_dn = jnp.logical_and(r < rows_n - 1, r <= c)
    has_rt = jnp.logical_and(active, c < cols_n - 1)
    has_lf = jnp.logical_and(r <= c, c > 0)

    up_dev, dn_dev = (r - 1, c), (r + 1, c)
    rt_dev, lf_dev = (r, c + 1), (r, c - 1)
    zh_dev = [(r, col_of(y, (zh + d) % ZH_N)) for d in (1, 2, 3)]
    y_up, y_dn = (y + 1) % Y_N, (y + Y_N - 1) % Y_N
    y_dev = [(r, col_of(y_up, zh)), (r, col_of(y_dn, zh))]
    core_dev = (row_of(zl, x, 1 - core), c)
    z_dev = (row_of(1 - zl, x, core), c)
    xp_dev = (row_of(zl, (x + 1) % X_N, core), c)
    xm_dev = (row_of(zl, (x + X_N - 1) % X_N, core), c)

    def remote(src, dst, send, recv, device):
        return pltpu.make_async_remote_copy(
            src_ref=src, dst_ref=dst, send_sem=send, recv_sem=recv, device_id=device, device_id_type=MESH
        )

    tile_in = pltpu.make_async_copy(h_ref, tile, in_sem.at[0])
    plan_in = pltpu.make_async_copy(plan_hbm, plan_ref, in_sem.at[1])
    plan_in.start()
    tile_in.start()

    barrier = pltpu.get_barrier_semaphore()
    around = [((r + step) % rows_n, c) for step in (1, rows_n - 1)] + [(r, (c + step) % cols_n) for step in (1, cols_n - 1)]
    peers = zh_dev + y_dev + [core_dev, z_dev, xp_dev, xm_dev] + around
    for device in peers:
        pl.semaphore_signal(barrier, inc=1, device_id=device, device_id_type=MESH)
    first_core = core == c % CORE_N
    is_root = r == c

    @pl.when(first_core)
    def _():
        @pl.loop(0, cols_n)
        def _(col):
            @pl.when(jnp.logical_or(r != c, col != c))
            def _():
                pl.semaphore_signal(barrier, inc=1, device_id=(c, col), device_id_type=MESH)

            @pl.when(col >= cols_n // 2)
            def _():
                before = (c + rows_n - 1) % rows_n
                pl.semaphore_signal(barrier, inc=1, device_id=(before, col), device_id_type=MESH)

    chips = rows_n // CORE_N
    expected = len(peers) + chips - jnp.where(is_root, 1, 0) + jnp.where(c >= cols_n // 2, chips, 0)
    pl.semaphore_wait(barrier, expected)

    def z_copy(d, at_zh):
        at = v_l.at[y, :, pl.ds(pl.multiple_of(at_zh * piece, piece), piece)]
        return remote(panel_ref, at, g_send.at[d], g_recv.at[d], zh_dev[d])

    own_copy = pltpu.make_async_copy(panel_ref, v_l.at[y, :, pl.ds(pl.multiple_of(zh * piece, piece), piece)], in_sem.at[2])
    for d in range(3):
        z_copy(d, zh).start()
    own_copy.start()

    def piece_target(n, step):
        at_zl, at_x = (zl + n // X_N) % 2, (x + n % X_N) % X_N
        row = row_of(at_zl, at_x, (r + step) % CORE_N)
        return row, (row, r + step), row - row % CORE_N <= r + step + 1

    def c_copy(n, col, device):
        at_y, at_zh = col // ZH_N, col % ZH_N
        at = v_r.at[at_y, :, pl.ds(pl.multiple_of(at_zh * piece, piece), piece)]
        return remote(panel_ref, at, c_send.at[n], c_recv.at[col], device)

    def d_copy(n, col, device):
        at_y, at_zh = col // ZH_N - Y_N // 2, col % ZH_N
        at = x_r.at[at_y, pl.ds(pl.multiple_of(at_zh * piece, piece), piece)]
        return remote(panel_ref.at[1], at, d_send.at[n], d_recv.at[col - cols_n // 2], device)

    self_copy = pltpu.make_async_copy(
        panel_ref, v_r.at[y, :, pl.ds(pl.multiple_of(zh * piece, piece), piece)], in_sem.at[3]
    )
    gives_bottom = jnp.logical_and(c >= cols_n // 2, r < rows_n - 1)
    served = r - core <= c + 1

    def pieces_out(act):
        for n in range(chips):
            row, device, wanted = piece_target(n, 0)

            @pl.when(jnp.logical_and(wanted, jnp.logical_or(row != r, c != r)))
            def _():
                act(c_copy(n, c, device))

        for n in range(chips):
            row, device, wanted = piece_target(n, 1)

            @pl.when(jnp.logical_and(wanted, gives_bottom))
            def _():
                act(d_copy(n, jnp.maximum(c, cols_n // 2), device))

    pieces_out(lambda copy: copy.start())

    @pl.when(is_root)
    def _():
        self_copy.start()

    @pl.when(jnp.logical_not(has_dn))
    def _():
        from_below[...] = jnp.zeros_like(from_below)

    @pl.when(jnp.logical_not(has_up))
    def _():
        from_above[...] = jnp.zeros_like(from_above)
        x_l[0:2] = jnp.zeros((2, h, h), F32)
        x_l[5] = jnp.zeros((h, h), F32)

    @pl.when(jnp.logical_not(has_rt))
    def _():
        from_right[...] = jnp.zeros_like(from_right)

    @pl.when(jnp.logical_not(has_lf))
    def _():
        from_left[...] = jnp.zeros_like(from_left)

    @pl.when(jnp.logical_not(has_lf))
    def _():
        x_r[5] = jnp.zeros((h, h), F32)

    @pl.when(c == 0)
    def _():
        x_r[0:2] = jnp.zeros((2, h, h), F32)

    def y_copy(side, at_y):
        block = v_l.at[at_y]
        return remote(block, block, y_send.at[side], y_recv.at[side], y_dev[side])

    def pass_copy(side, at_y):
        block = v_l.at[at_y, :, side * 2 * piece : (side + 1) * 2 * piece]
        return remote(block, block, f_send.at[side], f_recv.at[side], y_dev[side])

    own_copy.wait()
    for d in range(3):
        z_copy(d, (zh + ZH_N - 1 - d) % ZH_N).wait_recv()
    for side in range(2):
        y_copy(side, y).start()

    tile_in.wait()

    @pl.when(active)
    def _():
        @pl.loop(0, 8)
        def _(i):
            at = pl.ds(pl.multiple_of(i * h, h), h)
            high[at, :], low[at, :] = split(tile[at, :])

    sources = (y_dn, y_up)
    for side in range(2):
        y_copy(side, sources[side]).wait_recv()
        pass_copy(side, sources[side]).start()
    far = (y + 2) % Y_N
    for side in range(2):
        pass_copy(side, far).wait_recv()

    def bottom_copy():
        return remote(v_l.at[2:4, 1], x_l.at[0:2], n_send.at[0], n_recv.at[0], dn_dev)

    def factor_copy():
        return remote(x_l.at[4], x_l.at[5], n_send.at[1], n_recv.at[1], dn_dev)

    @pl.when(has_dn)
    def _():
        bottom_copy().start()

    plan_in.wait()

    def factors(v, index):
        at_row = lax.broadcasted_iota(jnp.int32, (h, h), 0)
        at_col = lax.broadcasted_iota(jnp.int32, (h, h), 1)
        eye = jnp.where(at_row == at_col, 1.0, 0.0).astype(F32)
        powers, results, scales = [], [], []
        for k in range(3):
            panel = jnp.concatenate([v[at, k] for at in range(4)], axis=0)
            gram = exact_dot(panel.T, panel)
            upper = jnp.where(at_row < at_col, gram, jnp.where(at_row == at_col, gram * 0.5, 0.0))
            diag = jnp.where(at_row == at_col, upper, 0.0)
            power = eye - upper * (1.0 / jnp.sum(diag, axis=1, keepdims=True))
            powers.append(power)
            results.append(eye + power)
            scales.append(1.0 / jnp.sum(diag, axis=0, keepdims=True))
        span = 2
        while span < h:
            powers = [exact_dot(power, power) for power in powers]
            results = [result + exact_dot(result, power) for result, power in zip(results, powers)]
            span = span * 2
        live = [
            plan_ref[0, index] > 0,
            jnp.logical_and(plan_ref[1, index] > 0, index < rows_n - 1),
            plan_ref[2, index] > 0,
        ]
        return [jnp.where(live[k], results[k] * scales[k], 0.0) for k in range(3)]

    @pl.when(active)
    def _():
        left_factors = factors(v_l, r)
        x_l[4] = left_factors[1]
        for k in range(3):
            f_h[k], f_l[k] = split(left_factors[k].T)

    @pl.when(has_dn)
    def _():
        factor_copy().start()

    @pl.when(has_up)
    def _():
        bottom_copy().wait_recv()

    def k_copy(at):
        return remote(v_r.at[at], v_r.at[at], k_send.at[at], k_recv.at[at], core_dev)

    def l_copy():
        return remote(x_r.at[0:2], x_r.at[0:2], k_send.at[Y_N], k_recv.at[Y_N], core_dev)

    has_before = jnp.logical_and(served, c > 0)

    @pl.when(jnp.logical_and(served, first_core))
    def _():
        @pl.loop(0, Y_N)
        def _(at):
            @pl.loop(0, ZH_N)
            def _(n):
                col = at * ZH_N + n

                @pl.when(jnp.logical_or(r != c, col != c))
                def _():
                    c_copy(0, col, core_dev).wait_recv()

                @pl.when(jnp.logical_and(r == c, col == c))
                def _():
                    self_copy.wait()

            k_copy(at).start()

    @pl.when(jnp.logical_and(has_before, first_core))
    def _():
        @pl.loop(cols_n // 2, cols_n)
        def _(col):
            d_copy(0, col, core_dev).wait_recv()

        l_copy().start()


    def operators(side, v, x):
        def top(k):
            return jnp.concatenate([v[0, k], v[1, k]], axis=0)

        def bottom(k):
            return jnp.concatenate([v[2, k], v[3, k]], axis=0)

        before = jnp.concatenate([x[0], x[1]], axis=0)
        pairs = [jnp.concatenate([top(0), before], axis=1), jnp.concatenate([bottom(0), top(2)], axis=1)]
        thin = [bottom(2), top(1)]
        for at in range(2):
            pair_h[2 * side + at], pair_l[2 * side + at] = split(pairs[at])
            thin_h[2 * side + at], thin_l[2 * side + at] = split(thin[at])
        first = exact_dot(before.T, top(0))
        second = exact_dot(top(2).T, bottom(0))
        cc_h[...], cc_l[...] = split(jnp.concatenate([first, second], axis=0))
        return pairs, thin

    def pair(at):
        return pair_h[at], pair_l[at]

    def thinner(at):
        return thin_h[at], thin_l[at]

    def turned(at):
        return turn_h[at], turn_l[at]

    def tthin(at):
        return tthin_h[at], tthin_l[at]

    def f_of(k):
        return f_h[k], f_l[k]

    def c_of():
        return cc_h[...], cc_l[...]

    band = [slice(i * b, (i + 1) * b) for i in range(4)]

    def band_of(i):
        return high[band[i], :], low[band[i], :]

    def lower_band(i, value):
        value = tile[band[i], :] - value
        tile[band[i], :] = value
        high[band[i], :], low[band[i], :] = split(value)

    def t_copy():
        return remote(t_own, from_above, row_send.at[0], row_recv.at[0], dn_dev)

    def p_copy():
        return remote(p_own, from_below, row_send.at[1], row_recv.at[1], up_dev)

    @pl.when(active)
    def _():
        pairs, thin = operators(0, v_l, x_l)
        for at in range(2):
            turn_h[at], turn_l[at] = split(pairs[at].T)
            tthin_h[at], tthin_l[at] = split(thin[at].T)
        t_own[...] = dot3(tthin(1), band_of(3))

    @pl.when(has_dn)
    def _():
        t_copy().start()


    @pl.when(active)
    def _():
        x0 = dot3(turned(0), band_of(0))
        x1 = dot3(turned(1), band_of(1))
        p_own[...] = x0[h:]
        t0_h[...], t0_l[...] = split(x0[:h] + x1[:h])
        t2_own[...] = x1[h:] + dot3(tthin(0), band_of(2))
        u0 = split(dot3(f_of(0), (t0_h[...], t0_l[...])))
        t0_h[...], t0_l[...] = u0
        shift = dot3(c_of(), u0)
        p_own[...] = p_own[...] - shift[:h]
        u2_h[...], u2_l[...] = split(dot3(f_of(2), split(t2_own[...] - shift[h:])))

    @pl.when(has_up)
    def _():
        p_copy().start()
        factor_copy().wait_recv()


    @pl.when(active)
    def _():
        u0, u2 = (t0_h[...], t0_l[...]), (u2_h[...], u2_l[...])
        lower_band(1, dot3(pair(1), join(u0, u2, 0)))
        lower_band(2, dot3(thinner(0), u2))
        f_h[3], f_l[3] = split(x_l[5].T)

    def st_copy(i):
        return remote(st_own.at[i], from_left.at[i], rt_send.at[i], rt_recv.at[i], rt_dev)

    def sb_copy(i):
        return remote(sb_own.at[i], from_right.at[i], lf_send.at[i], lf_recv.at[i], lf_dev)

    parts = [(slice(b, 3 * b),), (slice(0, b), slice(3 * b, 4 * b))]

    def out_copies(i):
        return [
            pltpu.make_async_copy(tile.at[at], out_ref.at[at], out_sem.at[i + n]) for n, at in enumerate(parts[i])
        ]

    def cut(i, j):
        return tuple(jnp.concatenate([ref[at, band[j]] for at in parts[i]], axis=0) for ref in (high, low))

    def lower_cols(i, j, value):
        done = 0
        for at in parts[i]:
            count = at.stop - at.start
            tile[at, band[j]] = tile[at, band[j]] - value[done : done + count]
            done = done + count

    def right_start(i):
        @pl.when(active)
        def _():
            st_own[i] = dot3(cut(i, 3), thinner(3))

        @pl.when(has_rt)
        def _():
            st_copy(i).start()

        @pl.when(active)
        def _():
            x0 = dot3(cut(i, 0), pair(2))
            x1 = dot3(cut(i, 1), pair(3))
            y0 = split(dot3(split(x0[:, :h] + x1[:, :h]), f_of(4)))
            y0_h[i], y0_l[i] = y0
            shift = dot3(y0, c_of(), turned=True)
            sb_own[i] = x0[:, h:] - shift[:, :h]
            y2_own[...] = x1[:, h:] - shift[:, h:]

        @pl.when(has_lf)
        def _():
            sb_copy(i).start()

    def right_middle(i):
        @pl.when(active)
        def _():
            y2_of = split(dot3(split(y2_own[...] + dot3(cut(i, 2), thinner(2))), f_of(6)))
            lower_cols(i, 1, dot3(join((y0_h[i], y0_l[i]), y2_of, 1), pair(3), turned=True))
            lower_cols(i, 2, dot3(y2_of, thinner(2), turned=True))

    def right_end(i):
        @pl.when(has_rt)
        def _():
            sb_copy(i).wait_recv()

        @pl.when(has_lf)
        def _():
            st_copy(i).wait_recv()

        @pl.when(active)
        def _():
            y1 = split(dot3(split(st_own[i] + from_right[i]), f_of(5)))
            y1p = split(dot3(split(from_left[i] + sb_own[i]), f_of(7)))
            lower_cols(i, 0, dot3(join((y0_h[i], y0_l[i]), y1p, 1), pair(2), turned=True))
            lower_cols(i, 3, dot3(y1, thinner(3), turned=True))

        for copy in out_copies(i):
            copy.start()

    @pl.when(jnp.logical_and(served, jnp.logical_not(first_core)))
    def _():
        @pl.loop(0, Y_N)
        def _(at):
            k_copy(at).wait_recv()

    @pl.when(jnp.logical_and(has_before, jnp.logical_not(first_core)))
    def _():
        l_copy().wait_recv()

    def m_copy():
        return remote(x_r.at[4], x_r.at[5], m_send.at[0], m_recv.at[0], rt_dev)

    @pl.when(active)
    def _():
        operators(1, v_r, x_r)
        right_factors = factors(v_r, c)
        x_r[4] = right_factors[1]
        for k in range(3):
            f_h[4 + k], f_l[4 + k] = split(right_factors[k])

    @pl.when(has_rt)
    def _():
        m_copy().start()

    right_start(0)

    @pl.when(has_dn)
    def _():
        p_copy().wait_recv()

    @pl.when(has_up)
    def _():
        t_copy().wait_recv()

    @pl.when(active)
    def _():
        u1 = split(dot3(f_of(1), split(t_own[...] + from_below[...])))
        u1p = split(dot3(f_of(3), split(from_above[...] + p_own[...])))
        lower_band(0, dot3(pair(0), join((t0_h[...], t0_l[...]), u1p, 0)))
        lower_band(3, dot3(thinner(1), u1))

    right_middle(0)
    right_start(1)
    right_middle(1)

    @pl.when(has_lf)
    def _():
        m_copy().wait_recv()

    @pl.when(active)
    def _():
        f_h[7], f_l[7] = split(x_r[5])

    right_end(0)
    right_end(1)

    for d in range(3):
        z_copy(d, zh).wait_send()
    for side in range(2):
        y_copy(side, y).wait_send()
        pass_copy(side, sources[side]).wait_send()

    @pl.when(has_dn)
    def _():
        bottom_copy().wait_send()
        factor_copy().wait_send()
        t_copy().wait_send()

    @pl.when(has_up)
    def _():
        p_copy().wait_send()

    pieces_out(lambda copy: copy.wait_send())

    @pl.when(jnp.logical_and(served, first_core))
    def _():
        @pl.loop(0, Y_N)
        def _(at):
            k_copy(at).wait_send()

    @pl.when(jnp.logical_and(has_before, first_core))
    def _():
        l_copy().wait_send()

    @pl.when(has_rt)
    def _():
        m_copy().wait_send()

    for i in range(2):

        @pl.when(has_rt)
        def _():
            st_copy(i).wait_send()

        @pl.when(has_lf)
        def _():
            sb_copy(i).wait_send()

        for copy in out_copies(i):
            copy.wait()


def solution(mesh):
    rows_n, cols_n = mesh.shape["row"], mesh.shape["col"]

    def on_device(matrix_tiles, panels, plan):
        size, refl = matrix_tiles.shape[-1], panels.shape[-1]
        b, h = size // 4, refl
        piece = panels.shape[3]
        vmem, dma = pltpu.VMEM, pltpu.SemaphoreType.DMA
        scratch = [
            pltpu.SMEM(plan.shape, jnp.int32),
            vmem((4, 3, h, h), F32), vmem((6, h, h), F32), vmem((4, 3, h, h), F32), vmem((6, h, h), F32),
            vmem((size, size), F32), vmem((size, size), BF16), vmem((size, size), BF16),
            vmem((4, b, b), BF16), vmem((4, b, b), BF16), vmem((4, b, h), BF16), vmem((4, b, h), BF16),
            vmem((2, b, b), BF16), vmem((2, b, b), BF16), vmem((2, h, b), BF16), vmem((2, h, b), BF16),
            vmem((8, h, h), BF16), vmem((8, h, h), BF16), vmem((b, h), BF16), vmem((b, h), BF16),
            vmem((h, size), BF16), vmem((h, size), BF16), vmem((h, size), F32), vmem((h, size), BF16), vmem((h, size), BF16),
            vmem((h, size), F32), vmem((h, size), F32), vmem((h, size), F32), vmem((h, size), F32),
            vmem((2, 2 * b, h), F32), vmem((2, 2 * b, h), F32), vmem((2, 2 * b, h), F32), vmem((2, 2 * b, h), F32),
            vmem((2, 2 * b, h), BF16), vmem((2, 2 * b, h), BF16), vmem((2 * b, h), F32),
            dma((4,)), dma((3,)),
            dma((3,)), dma((3,)), dma((2,)), dma((2,)), dma((2,)), dma((2,)), dma((2,)), dma((2,)),
            dma((8,)), dma((16,)), dma((8,)), dma((8,)), dma((5,)), dma((5,)), dma((1,)), dma((1,)), dma((2,)), dma((2,)), dma((2,)), dma((2,)), dma((2,)), dma((2,)),
        ]
        result = pl.pallas_call(
            functools.partial(kernel, rows_n, cols_n, b),
            out_shape=jax.ShapeDtypeStruct((size, size), F32),
            in_specs=[pl.BlockSpec(memory_space=pltpu.HBM)] * 3,
            out_specs=pl.BlockSpec(memory_space=pl.ANY),
            scratch_shapes=scratch,
            compiler_params=pltpu.CompilerParams(
                collective_id=0, has_side_effects=True, vmem_limit_bytes=48 * 1024 * 1024
            ),
        )(matrix_tiles.reshape(size, size), panels.reshape(3, piece, refl), plan)
        return result.reshape(matrix_tiles.shape)

    placed = (P(None, "row", None, "col", None, None), P(None, None, "row", "col", None), P())
    return jax.shard_map(
        on_device,
        mesh=mesh,
        in_specs=placed,
        out_specs=P(None, "row", None, "col", None, None),
        check_vma=False,
    )
```

```python
import functools

import jax
import jax.numpy as jnp
from jax import lax
from jax.experimental import pallas as pl
from jax.experimental.pallas import tpu as pltpu
from jax.sharding import PartitionSpec as P

MESH = pl.DeviceIdType.MESH
F32 = jnp.float32
BF16 = jnp.bfloat16

X_N, CORE_N, Y_N, ZH_N = 4, 2, 4, 4


def split(value):
    high = value.astype(BF16)
    low = (value - high.astype(F32)).astype(BF16)
    return high, low


def dot3(left, right, turned=False):
    side = 1 if turned else 0
    a = jnp.concatenate([left[0], left[0], left[1]], axis=1)
    z = jnp.concatenate([right[0], right[1], right[0]], axis=side)
    return lax.dot_general(a, z, (((1,), (side,)), ((), ())), preferred_element_type=F32)


def join(first, second, axis):
    return tuple(jnp.concatenate([a, z], axis=axis) for a, z in zip(first, second))


def exact_dot(left, right):
    return jnp.dot(left, right, precision=lax.Precision.HIGHEST, preferred_element_type=F32)


def kernel(
    rows_n, cols_n, b, h_ref, panel_ref, plan_hbm, out_ref,
    plan_ref, v_l, x_l, v_r, x_r, tile, high, low, pair_h, pair_l, thin_h, thin_l, turn_h, turn_l, tthin_h, tthin_l,
    f_h, f_l, cc_h, cc_l, t0_h, t0_l, t2_own, u2_h, u2_l, t_own, p_own, from_below, from_above,
    st_own, sb_own, from_right, from_left, y0_h, y0_l, y2_own,
    in_sem, out_sem, g_send, g_recv, y_send, y_recv, f_send, f_recv, n_send, n_recv,
    c_send, c_recv, d_send, d_recv, k_send, k_recv, m_send, m_recv, row_send, row_recv, rt_send, rt_recv, lf_send, lf_recv, pass_send,
):
    h = b // 2
    piece = 2 * b // cols_n
    r = lax.axis_index("row")
    c = lax.axis_index("col")
    zl, x, core = r // (X_N * CORE_N), (r // CORE_N) % X_N, r % CORE_N
    y, zh = c // ZH_N, c % ZH_N

    def row_of(zl, x, core):
        return zl * (X_N * CORE_N) + x * CORE_N + core

    def col_of(y, zh):
        return y * ZH_N + zh

    active = r <= c + 1
    has_up = jnp.logical_and(active, r > 0)
    has_dn = jnp.logical_and(r < rows_n - 1, r <= c)
    has_rt = jnp.logical_and(active, c < cols_n - 1)
    has_lf = jnp.logical_and(r <= c, c > 0)

    up_dev, dn_dev = (r - 1, c), (r + 1, c)
    rt_dev, lf_dev = (r, c + 1), (r, c - 1)
    zh_dev = [(r, col_of(y, (zh + d) % ZH_N)) for d in (1, 2, 3)]
    y_up, y_dn = (y + 1) % Y_N, (y + Y_N - 1) % Y_N
    y_dev = [(r, col_of(y_up, zh)), (r, col_of(y_dn, zh))]
    core_dev = (row_of(zl, x, 1 - core), c)

    def relay_col(col):
        return col_of(Y_N - 1 - col // ZH_N, col % ZH_N)

    def relayed(col):
        low_rows = jnp.logical_and(r >= rows_n // 2, r > relay_col(col) + 1)
        return jnp.logical_and(low_rows, col // ZH_N >= Y_N // 2)

    rt_relay = jnp.logical_and(zh < ZH_N - 1, relayed(c))
    lf_relay = jnp.logical_and(zh > 0, relayed(c))
    rt_first = (r, jnp.where(rt_relay, relay_col(c), c + 1))
    lf_first = (r, jnp.where(lf_relay, relay_col(c), c - 1))
    served_col = relay_col(c)
    is_relay = jnp.logical_and(y < Y_N // 2, relayed(served_col))
    pass_rt = jnp.logical_and(is_relay, jnp.logical_and(zh < ZH_N - 1, r <= served_col + 1))
    pass_lf = jnp.logical_and(is_relay, jnp.logical_and(zh > 0, r <= served_col))

    def remote(src, dst, send, recv, device):
        return pltpu.make_async_remote_copy(
            src_ref=src, dst_ref=dst, send_sem=send, recv_sem=recv, device_id=device, device_id_type=MESH
        )

    tile_in = pltpu.make_async_copy(h_ref, tile, in_sem.at[0])
    plan_in = pltpu.make_async_copy(plan_hbm, plan_ref, in_sem.at[1])
    plan_in.start()
    tile_in.start()

    barrier = pltpu.get_barrier_semaphore()
    around = [((r + step) % rows_n, c) for step in (1, rows_n - 1)] + [(r, (c + step) % cols_n) for step in (1, cols_n - 1)]
    mirror = Y_N - 1 - y
    relay_peers = [(r, col_of(mirror, (zh + step) % ZH_N)) for step in (1, ZH_N - 1)]
    peers = zh_dev + y_dev + [core_dev] + around + relay_peers
    for device in peers:
        pl.semaphore_signal(barrier, inc=1, device_id=device, device_id_type=MESH)
    first_core = core == c % CORE_N
    is_root = r == c

    @pl.when(first_core)
    def _():
        @pl.loop(0, cols_n)
        def _(col):
            @pl.when(jnp.logical_or(r != c, col != c))
            def _():
                pl.semaphore_signal(barrier, inc=1, device_id=(c, col), device_id_type=MESH)

            @pl.when(col >= cols_n // 2)
            def _():
                before = (c + rows_n - 1) % rows_n
                pl.semaphore_signal(barrier, inc=1, device_id=(before, col), device_id_type=MESH)

    chips = rows_n // CORE_N
    expected = len(peers) + chips - jnp.where(is_root, 1, 0) + jnp.where(c >= cols_n // 2, chips, 0)
    pl.semaphore_wait(barrier, expected)

    def z_copy(d, at_zh):
        at = v_l.at[y, :, pl.ds(pl.multiple_of(at_zh * piece, piece), piece)]
        return remote(panel_ref, at, g_send.at[d], g_recv.at[d], zh_dev[d])

    own_copy = pltpu.make_async_copy(panel_ref, v_l.at[y, :, pl.ds(pl.multiple_of(zh * piece, piece), piece)], in_sem.at[2])
    for d in range(3):
        z_copy(d, zh).start()
    own_copy.start()

    def piece_target(n, step):
        at_zl, at_x = (zl + n // X_N) % 2, (x + n % X_N) % X_N
        row = row_of(at_zl, at_x, (r + step) % CORE_N)
        return row, (row, r + step), row - row % CORE_N <= r + step + 1

    def c_copy(n, col, device):
        at_y, at_zh = col // ZH_N, col % ZH_N
        at = v_r.at[at_y, :, pl.ds(pl.multiple_of(at_zh * piece, piece), piece)]
        return remote(panel_ref, at, c_send.at[n], c_recv.at[col], device)

    def d_copy(n, col, device):
        at_y, at_zh = col // ZH_N - Y_N // 2, col % ZH_N
        at = x_r.at[at_y, pl.ds(pl.multiple_of(at_zh * piece, piece), piece)]
        return remote(panel_ref.at[1], at, d_send.at[n], d_recv.at[col - cols_n // 2], device)

    self_copy = pltpu.make_async_copy(
        panel_ref, v_r.at[y, :, pl.ds(pl.multiple_of(zh * piece, piece), piece)], in_sem.at[3]
    )
    gives_bottom = jnp.logical_and(c >= cols_n // 2, r < rows_n - 1)
    served = r - core <= c + 1

    def pieces_out(act):
        for n in range(chips):
            row, device, wanted = piece_target(n, 0)

            @pl.when(jnp.logical_and(wanted, jnp.logical_or(row != r, c != r)))
            def _():
                act(c_copy(n, c, device))

        for n in range(chips):
            row, device, wanted = piece_target(n, 1)

            @pl.when(jnp.logical_and(wanted, gives_bottom))
            def _():
                act(d_copy(n, jnp.maximum(c, cols_n // 2), device))

    pieces_out(lambda copy: copy.start())

    @pl.when(is_root)
    def _():
        self_copy.start()

    @pl.when(jnp.logical_and(active, jnp.logical_not(has_dn)))
    def _():
        from_below[...] = jnp.zeros_like(from_below)

    @pl.when(jnp.logical_and(active, jnp.logical_not(has_up)))
    def _():
        from_above[...] = jnp.zeros_like(from_above)
        x_l[0:2] = jnp.zeros((2, h, h), F32)
        x_l[5] = jnp.zeros((h, h), F32)

    @pl.when(jnp.logical_and(active, jnp.logical_not(has_rt)))
    def _():
        from_right[...] = jnp.zeros_like(from_right)

    @pl.when(jnp.logical_and(active, jnp.logical_not(has_lf)))
    def _():
        from_left[...] = jnp.zeros_like(from_left)

    @pl.when(jnp.logical_and(active, jnp.logical_not(has_lf)))
    def _():
        x_r[5] = jnp.zeros((h, h), F32)

    @pl.when(c == 0)
    def _():
        x_r[0:2] = jnp.zeros((2, h, h), F32)

    def y_copy(side, at_y):
        block = v_l.at[at_y]
        return remote(block, block, y_send.at[side], y_recv.at[side], y_dev[side])

    def pass_copy(side, at_y):
        block = v_l.at[at_y, :, side * 2 * piece : (side + 1) * 2 * piece]
        return remote(block, block, f_send.at[side], f_recv.at[side], y_dev[side])

    own_copy.wait()
    for d in range(3):
        z_copy(d, (zh + ZH_N - 1 - d) % ZH_N).wait_recv()
    for side in range(2):
        y_copy(side, y).start()

    tile_in.wait()

    @pl.when(active)
    def _():
        @pl.loop(0, 8)
        def _(i):
            at = pl.ds(pl.multiple_of(i * h, h), h)
            high[at, :], low[at, :] = split(tile[at, :])

    sources = (y_dn, y_up)
    for side in range(2):
        y_copy(side, sources[side]).wait_recv()
        pass_copy(side, sources[side]).start()
    far = (y + 2) % Y_N
    for side in range(2):
        pass_copy(side, far).wait_recv()

    def bottom_copy():
        return remote(v_l.at[2:4, 1], x_l.at[0:2], n_send.at[0], n_recv.at[0], dn_dev)

    def factor_copy():
        return remote(x_l.at[4], x_l.at[5], n_send.at[1], n_recv.at[1], dn_dev)

    @pl.when(has_dn)
    def _():
        bottom_copy().start()

    plan_in.wait()

    def factors(v, index):
        at_row = lax.broadcasted_iota(jnp.int32, (h, h), 0)
        at_col = lax.broadcasted_iota(jnp.int32, (h, h), 1)
        eye = jnp.where(at_row == at_col, 1.0, 0.0).astype(F32)
        powers, results, scales = [], [], []
        for k in range(3):
            panel = jnp.concatenate([v[at, k] for at in range(4)], axis=0)
            gram = exact_dot(panel.T, panel)
            upper = jnp.where(at_row < at_col, gram, jnp.where(at_row == at_col, gram * 0.5, 0.0))
            diag = jnp.where(at_row == at_col, upper, 0.0)
            power = eye - upper * (1.0 / jnp.sum(diag, axis=1, keepdims=True))
            powers.append(power)
            results.append(eye + power)
            scales.append(1.0 / jnp.sum(diag, axis=0, keepdims=True))
        span = 2
        while span < h:
            powers = [exact_dot(power, power) for power in powers]
            results = [result + exact_dot(result, power) for result, power in zip(results, powers)]
            span = span * 2
        live = [
            plan_ref[0, index] > 0,
            jnp.logical_and(plan_ref[1, index] > 0, index < rows_n - 1),
            plan_ref[2, index] > 0,
        ]
        return [jnp.where(live[k], results[k] * scales[k], 0.0) for k in range(3)]

    @pl.when(active)
    def _():
        left_factors = factors(v_l, r)
        x_l[4] = left_factors[1]
        for k in range(3):
            f_h[k], f_l[k] = split(left_factors[k].T)

    @pl.when(has_dn)
    def _():
        factor_copy().start()

    @pl.when(has_up)
    def _():
        bottom_copy().wait_recv()

    def operators(side, v, x):
        def top(k):
            return jnp.concatenate([v[0, k], v[1, k]], axis=0)

        def bottom(k):
            return jnp.concatenate([v[2, k], v[3, k]], axis=0)

        before = jnp.concatenate([x[0], x[1]], axis=0)
        pairs = [jnp.concatenate([top(0), before], axis=1), jnp.concatenate([bottom(0), top(2)], axis=1)]
        thin = [bottom(2), top(1)]
        for at in range(2):
            pair_h[2 * side + at], pair_l[2 * side + at] = split(pairs[at])
            thin_h[2 * side + at], thin_l[2 * side + at] = split(thin[at])
        first = exact_dot(before.T, top(0))
        second = exact_dot(top(2).T, bottom(0))
        cc_h[...], cc_l[...] = split(jnp.concatenate([first, second], axis=0))
        return pairs, thin

    def pair(at):
        return pair_h[at], pair_l[at]

    def thinner(at):
        return thin_h[at], thin_l[at]

    def turned(at):
        return turn_h[at], turn_l[at]

    def tthin(at):
        return tthin_h[at], tthin_l[at]

    def f_of(k):
        return f_h[k], f_l[k]

    def c_of():
        return cc_h[...], cc_l[...]

    band = [slice(i * b, (i + 1) * b) for i in range(4)]

    def band_of(i):
        return high[band[i], :], low[band[i], :]

    def lower_band(i, value):
        value = tile[band[i], :] - value
        tile[band[i], :] = value
        high[band[i], :], low[band[i], :] = split(value)

    def t_copy():
        return remote(t_own, from_above, row_send.at[0], row_recv.at[0], dn_dev)

    def p_copy():
        return remote(p_own, from_below, row_send.at[1], row_recv.at[1], up_dev)

    @pl.when(active)
    def _():
        pairs, thin = operators(0, v_l, x_l)
        for at in range(2):
            turn_h[at], turn_l[at] = split(pairs[at].T)
            tthin_h[at], tthin_l[at] = split(thin[at].T)
        t_own[...] = dot3(tthin(1), band_of(3))

    @pl.when(has_dn)
    def _():
        t_copy().start()


    @pl.when(active)
    def _():
        x0 = dot3(turned(0), band_of(0))
        x1 = dot3(turned(1), band_of(1))
        p_own[...] = x0[h:]
        t0_h[...], t0_l[...] = split(x0[:h] + x1[:h])
        t2_own[...] = x1[h:] + dot3(tthin(0), band_of(2))
        u0 = split(dot3(f_of(0), (t0_h[...], t0_l[...])))
        t0_h[...], t0_l[...] = u0
        shift = dot3(c_of(), u0)
        p_own[...] = p_own[...] - shift[:h]
        u2_h[...], u2_l[...] = split(dot3(f_of(2), split(t2_own[...] - shift[h:])))

    @pl.when(has_up)
    def _():
        p_copy().start()

    def k_copy(at):
        return remote(v_r.at[at], v_r.at[at], k_send.at[at], k_recv.at[at], core_dev)

    def l_copy():
        return remote(x_r.at[0:2], x_r.at[0:2], k_send.at[Y_N], k_recv.at[Y_N], core_dev)

    has_before = jnp.logical_and(served, c > 0)

    @pl.when(jnp.logical_and(served, first_core))
    def _():
        @pl.loop(0, Y_N)
        def _(at):
            @pl.loop(0, ZH_N)
            def _(n):
                col = at * ZH_N + n

                @pl.when(jnp.logical_or(r != c, col != c))
                def _():
                    c_copy(0, col, core_dev).wait_recv()

                @pl.when(jnp.logical_and(r == c, col == c))
                def _():
                    self_copy.wait()

            k_copy(at).start()

    @pl.when(jnp.logical_and(has_before, first_core))
    def _():
        @pl.loop(cols_n // 2, cols_n)
        def _(col):
            d_copy(0, col, core_dev).wait_recv()

        l_copy().start()


    @pl.when(has_up)
    def _():
        factor_copy().wait_recv()


    @pl.when(active)
    def _():
        u0, u2 = (t0_h[...], t0_l[...]), (u2_h[...], u2_l[...])
        lower_band(1, dot3(pair(1), join(u0, u2, 0)))
        lower_band(2, dot3(thinner(0), u2))
        f_h[3], f_l[3] = split(x_l[5].T)

    def st_copy(i):
        return remote(st_own.at[i], from_left.at[i], rt_send.at[i], rt_recv.at[i], rt_dev if i else rt_first)

    def sb_copy(i):
        return remote(sb_own.at[i], from_right.at[i], lf_send.at[i], lf_recv.at[i], lf_dev if i else lf_first)

    parts = [(slice(b, 3 * b),), (slice(0, b), slice(3 * b, 4 * b))]

    def out_copies(i):
        return [
            pltpu.make_async_copy(tile.at[at], out_ref.at[at], out_sem.at[i + n]) for n, at in enumerate(parts[i])
        ]

    def cut(i, j):
        return tuple(jnp.concatenate([ref[at, band[j]] for at in parts[i]], axis=0) for ref in (high, low))

    def lower_cols(i, j, value):
        done = 0
        for at in parts[i]:
            count = at.stop - at.start
            tile[at, band[j]] = tile[at, band[j]] - value[done : done + count]
            done = done + count

    def right_first(i):
        @pl.when(active)
        def _():
            st_own[i] = dot3(cut(i, 3), thinner(3))

        @pl.when(has_rt)
        def _():
            st_copy(i).start()

    def right_start(i):
        @pl.when(active)
        def _():
            x0 = dot3(cut(i, 0), pair(2))
            x1 = dot3(cut(i, 1), pair(3))
            y0 = split(dot3(split(x0[:, :h] + x1[:, :h]), f_of(4)))
            y0_h[i], y0_l[i] = y0
            shift = dot3(y0, c_of(), turned=True)
            sb_own[i] = x0[:, h:] - shift[:, :h]
            y2_own[...] = x1[:, h:] - shift[:, h:]

        @pl.when(has_lf)
        def _():
            sb_copy(i).start()

    def right_middle(i):
        @pl.when(active)
        def _():
            y2_of = split(dot3(split(y2_own[...] + dot3(cut(i, 2), thinner(2))), f_of(6)))
            lower_cols(i, 1, dot3(join((y0_h[i], y0_l[i]), y2_of, 1), pair(3), turned=True))
            lower_cols(i, 2, dot3(y2_of, thinner(2), turned=True))

    def right_end(i):
        @pl.when(has_rt)
        def _():
            sb_copy(i).wait_recv()

        @pl.when(has_lf)
        def _():
            st_copy(i).wait_recv()

        @pl.when(active)
        def _():
            y1 = split(dot3(split(st_own[i] + from_right[i]), f_of(5)))
            y1p = split(dot3(split(from_left[i] + sb_own[i]), f_of(7)))
            lower_cols(i, 0, dot3(join((y0_h[i], y0_l[i]), y1p, 1), pair(2), turned=True))
            lower_cols(i, 3, dot3(y1, thinner(3), turned=True))

        for copy in out_copies(i):
            copy.start()

    @pl.when(jnp.logical_and(served, jnp.logical_not(first_core)))
    def _():
        @pl.loop(0, Y_N)
        def _(at):
            k_copy(at).wait_recv()

    @pl.when(jnp.logical_and(has_before, jnp.logical_not(first_core)))
    def _():
        l_copy().wait_recv()

    def m_copy():
        return remote(x_r.at[4], x_r.at[5], m_send.at[0], m_recv.at[0], rt_dev)

    @pl.when(active)
    def _():
        operators(1, v_r, x_r)

    right_first(0)

    @pl.when(active)
    def _():
        right_factors = factors(v_r, c)
        x_r[4] = right_factors[1]
        for k in range(3):
            f_h[4 + k], f_l[4 + k] = split(right_factors[k])

    relay_copies = [
        (pass_rt, st_copy, remote(from_left.at[0], from_left.at[0], pass_send.at[0], rt_recv.at[0], (r, served_col + 1))),
        (pass_lf, sb_copy, remote(from_right.at[0], from_right.at[0], pass_send.at[1], lf_recv.at[0], (r, served_col - 1))),
    ]
    for there, arrived, onward in relay_copies:

        @pl.when(there)
        def _():
            arrived(0).wait_recv()
            onward.start()

    right_start(0)

    @pl.when(has_rt)
    def _():
        m_copy().start()


    @pl.when(has_dn)
    def _():
        p_copy().wait_recv()

    @pl.when(has_up)
    def _():
        t_copy().wait_recv()

    @pl.when(active)
    def _():
        u1 = split(dot3(f_of(1), split(t_own[...] + from_below[...])))
        u1p = split(dot3(f_of(3), split(from_above[...] + p_own[...])))
        lower_band(0, dot3(pair(0), join((t0_h[...], t0_l[...]), u1p, 0)))
        lower_band(3, dot3(thinner(1), u1))

    right_middle(0)
    right_first(1)
    right_start(1)
    right_middle(1)

    @pl.when(has_lf)
    def _():
        m_copy().wait_recv()

    @pl.when(active)
    def _():
        f_h[7], f_l[7] = split(x_r[5])

    right_end(0)
    right_end(1)

    for d in range(3):
        z_copy(d, zh).wait_send()
    for side in range(2):
        y_copy(side, y).wait_send()
        pass_copy(side, sources[side]).wait_send()

    @pl.when(has_dn)
    def _():
        bottom_copy().wait_send()
        factor_copy().wait_send()
        t_copy().wait_send()

    @pl.when(has_up)
    def _():
        p_copy().wait_send()

    pieces_out(lambda copy: copy.wait_send())
    for there, _, onward in relay_copies:

        @pl.when(there)
        def _():
            onward.wait_send()

    @pl.when(jnp.logical_and(served, first_core))
    def _():
        @pl.loop(0, Y_N)
        def _(at):
            k_copy(at).wait_send()

    @pl.when(jnp.logical_and(has_before, first_core))
    def _():
        l_copy().wait_send()

    @pl.when(has_rt)
    def _():
        m_copy().wait_send()

    for i in range(2):

        @pl.when(has_rt)
        def _():
            st_copy(i).wait_send()

        @pl.when(has_lf)
        def _():
            sb_copy(i).wait_send()

        for copy in out_copies(i):
            copy.wait()


def solution(mesh):
    rows_n, cols_n = mesh.shape["row"], mesh.shape["col"]

    def on_device(matrix_tiles, panels, plan):
        size, refl = matrix_tiles.shape[-1], panels.shape[-1]
        b, h = size // 4, refl
        piece = panels.shape[3]
        vmem, dma = pltpu.VMEM, pltpu.SemaphoreType.DMA
        scratch = [
            pltpu.SMEM(plan.shape, jnp.int32),
            vmem((4, 3, h, h), F32), vmem((6, h, h), F32), vmem((4, 3, h, h), F32), vmem((6, h, h), F32),
            vmem((size, size), F32), vmem((size, size), BF16), vmem((size, size), BF16),
            vmem((4, b, b), BF16), vmem((4, b, b), BF16), vmem((4, b, h), BF16), vmem((4, b, h), BF16),
            vmem((2, b, b), BF16), vmem((2, b, b), BF16), vmem((2, h, b), BF16), vmem((2, h, b), BF16),
            vmem((8, h, h), BF16), vmem((8, h, h), BF16), vmem((b, h), BF16), vmem((b, h), BF16),
            vmem((h, size), BF16), vmem((h, size), BF16), vmem((h, size), F32), vmem((h, size), BF16), vmem((h, size), BF16),
            vmem((h, size), F32), vmem((h, size), F32), vmem((h, size), F32), vmem((h, size), F32),
            vmem((2, 2 * b, h), F32), vmem((2, 2 * b, h), F32), vmem((2, 2 * b, h), F32), vmem((2, 2 * b, h), F32),
            vmem((2, 2 * b, h), BF16), vmem((2, 2 * b, h), BF16), vmem((2 * b, h), F32),
            dma((4,)), dma((3,)),
            dma((3,)), dma((3,)), dma((2,)), dma((2,)), dma((2,)), dma((2,)), dma((2,)), dma((2,)),
            dma((8,)), dma((16,)), dma((8,)), dma((8,)), dma((5,)), dma((5,)), dma((1,)), dma((1,)), dma((2,)), dma((2,)), dma((2,)), dma((2,)), dma((2,)), dma((2,)), dma((2,)),
        ]
        result = pl.pallas_call(
            functools.partial(kernel, rows_n, cols_n, b),
            out_shape=jax.ShapeDtypeStruct((size, size), F32),
            in_specs=[pl.BlockSpec(memory_space=pltpu.HBM)] * 3,
            out_specs=pl.BlockSpec(memory_space=pl.ANY),
            scratch_shapes=scratch,
            compiler_params=pltpu.CompilerParams(
                collective_id=0, has_side_effects=True, vmem_limit_bytes=48 * 1024 * 1024
            ),
        )(matrix_tiles.reshape(size, size), panels.reshape(3, piece, refl), plan)
        return result.reshape(matrix_tiles.shape)

    placed = (P(None, "row", None, "col", None, None), P(None, None, "row", "col", None), P())
    return jax.shard_map(
        on_device,
        mesh=mesh,
        in_specs=placed,
        out_specs=P(None, "row", None, "col", None, None),
        check_vma=False,
    )
```

```python
import functools

import jax
import jax.numpy as jnp
from jax import lax
from jax.experimental import pallas as pl
from jax.experimental.pallas import tpu as pltpu
from jax.sharding import PartitionSpec as P

MESH = pl.DeviceIdType.MESH
F32 = jnp.float32
BF16 = jnp.bfloat16

X_N, CORE_N, Y_N, ZH_N = 4, 2, 4, 4


def split(value):
    high = value.astype(BF16)
    low = (value - high.astype(F32)).astype(BF16)
    return high, low


def dot3(left, right, turned=False):
    side = 1 if turned else 0
    a = jnp.concatenate([left[0], left[0], left[1]], axis=1)
    z = jnp.concatenate([right[0], right[1], right[0]], axis=side)
    return lax.dot_general(a, z, (((1,), (side,)), ((), ())), preferred_element_type=F32)


def join(first, second, axis):
    return tuple(jnp.concatenate([a, z], axis=axis) for a, z in zip(first, second))


def exact_dot(left, right):
    return jnp.dot(left, right, precision=lax.Precision.HIGHEST, preferred_element_type=F32)


def kernel(
    rows_n, cols_n, b, h_ref, panel_ref, plan_hbm, out_ref,
    plan_ref, v_l, x_l, v_r, x_r, tile, high, low, pair_h, pair_l, thin_h, thin_l, turn_h, turn_l, tthin_h, tthin_l,
    f_h, f_l, cc_h, cc_l, t0_h, t0_l, t2_own, u2_h, u2_l, t_own, p_own, from_below, from_above,
    st_own, sb_own, from_right, from_left, y0_h, y0_l, y2_own,
    in_sem, out_sem, g_send, g_recv, y_send, y_recv, f_send, f_recv, n_send, n_recv,
    c_send, c_recv, d_send, d_recv, k_send, k_recv, m_send, m_recv, row_send, row_recv, rt_send, rt_recv, lf_send, lf_recv, pass_send,
):
    h = b // 2
    piece = 2 * b // cols_n
    r = lax.axis_index("row")
    c = lax.axis_index("col")
    zl, x, core = r // (X_N * CORE_N), (r // CORE_N) % X_N, r % CORE_N
    y, zh = c // ZH_N, c % ZH_N

    def row_of(zl, x, core):
        return zl * (X_N * CORE_N) + x * CORE_N + core

    def col_of(y, zh):
        return y * ZH_N + zh

    active = r <= c + 1
    has_up = jnp.logical_and(active, r > 0)
    has_dn = jnp.logical_and(r < rows_n - 1, r <= c)
    has_rt = jnp.logical_and(active, c < cols_n - 1)
    has_lf = jnp.logical_and(r <= c, c > 0)

    up_dev, dn_dev = (r - 1, c), (r + 1, c)
    rt_dev, lf_dev = (r, c + 1), (r, c - 1)
    zh_dev = [(r, col_of(y, (zh + d) % ZH_N)) for d in (1, 2, 3)]
    y_up, y_dn = (y + 1) % Y_N, (y + Y_N - 1) % Y_N
    y_dev = [(r, col_of(y_up, zh)), (r, col_of(y_dn, zh))]
    core_dev = (row_of(zl, x, 1 - core), c)

    def relay_col(col):
        return col_of(Y_N - 1 - col // ZH_N, col % ZH_N)

    def relayed(col):
        low_rows = jnp.logical_and(r >= rows_n // 2, r > relay_col(col) + 1)
        return jnp.logical_and(low_rows, col // ZH_N >= Y_N // 2)

    rt_relay = jnp.logical_and(zh < ZH_N - 1, relayed(c))
    lf_relay = jnp.logical_and(zh > 0, relayed(c))
    rt_first = (r, jnp.where(rt_relay, relay_col(c), c + 1))
    lf_first = (r, jnp.where(lf_relay, relay_col(c), c - 1))
    served_col = relay_col(c)
    is_relay = jnp.logical_and(y < Y_N // 2, relayed(served_col))
    pass_rt = jnp.logical_and(is_relay, jnp.logical_and(zh < ZH_N - 1, r <= served_col + 1))
    pass_lf = jnp.logical_and(is_relay, jnp.logical_and(zh > 0, r <= served_col))

    def remote(src, dst, send, recv, device):
        return pltpu.make_async_remote_copy(
            src_ref=src, dst_ref=dst, send_sem=send, recv_sem=recv, device_id=device, device_id_type=MESH
        )

    tile_in = pltpu.make_async_copy(h_ref, tile, in_sem.at[0])
    plan_in = pltpu.make_async_copy(plan_hbm, plan_ref, in_sem.at[1])
    plan_in.start()
    tile_in.start()

    barrier = pltpu.get_barrier_semaphore()
    around = [((r + step) % rows_n, c) for step in (1, rows_n - 1)] + [(r, (c + step) % cols_n) for step in (1, cols_n - 1)]
    mirror = Y_N - 1 - y
    relay_peers = [(r, col_of(mirror, (zh + step) % ZH_N)) for step in (1, ZH_N - 1)]
    peers = zh_dev + y_dev + [core_dev] + around + relay_peers
    for device in peers:
        pl.semaphore_signal(barrier, inc=1, device_id=device, device_id_type=MESH)
    first_core = core == c % CORE_N
    is_root = r == c

    @pl.when(first_core)
    def _():
        @pl.loop(0, cols_n)
        def _(col):
            @pl.when(jnp.logical_or(r != c, col != c))
            def _():
                pl.semaphore_signal(barrier, inc=1, device_id=(c, col), device_id_type=MESH)

            @pl.when(col >= cols_n // 2)
            def _():
                before = (c + rows_n - 1) % rows_n
                pl.semaphore_signal(barrier, inc=1, device_id=(before, col), device_id_type=MESH)

    chips = rows_n // CORE_N
    expected = len(peers) + chips - jnp.where(is_root, 1, 0) + jnp.where(c >= cols_n // 2, chips, 0)
    pl.semaphore_wait(barrier, expected)

    def z_copy(d, at_zh):
        at = v_l.at[y, :, pl.ds(pl.multiple_of(at_zh * piece, piece), piece)]
        return remote(panel_ref, at, g_send.at[d], g_recv.at[d], zh_dev[d])

    own_copy = pltpu.make_async_copy(panel_ref, v_l.at[y, :, pl.ds(pl.multiple_of(zh * piece, piece), piece)], in_sem.at[2])
    for d in range(3):
        z_copy(d, zh).start()
    own_copy.start()

    def piece_target(n, step):
        at_zl, at_x = (zl + n // X_N) % 2, (x + n % X_N) % X_N
        row = row_of(at_zl, at_x, (r + step) % CORE_N)
        return row, (row, r + step), row - row % CORE_N <= r + step + 1

    def c_copy(n, col, device):
        at_y, at_zh = col // ZH_N, col % ZH_N
        at = v_r.at[at_y, :, pl.ds(pl.multiple_of(at_zh * piece, piece), piece)]
        return remote(panel_ref, at, c_send.at[n], c_recv.at[col], device)

    def d_copy(n, col, device):
        at_y, at_zh = col // ZH_N - Y_N // 2, col % ZH_N
        at = x_r.at[at_y, pl.ds(pl.multiple_of(at_zh * piece, piece), piece)]
        return remote(panel_ref.at[1], at, d_send.at[n], d_recv.at[col - cols_n // 2], device)

    self_copy = pltpu.make_async_copy(
        panel_ref, v_r.at[y, :, pl.ds(pl.multiple_of(zh * piece, piece), piece)], in_sem.at[3]
    )
    gives_bottom = jnp.logical_and(c >= cols_n // 2, r < rows_n - 1)
    served = r - core <= c + 1

    def pieces_out(act):
        for n in range(chips):
            row, device, wanted = piece_target(n, 0)

            @pl.when(jnp.logical_and(wanted, jnp.logical_or(row != r, c != r)))
            def _():
                act(c_copy(n, c, device))

        for n in range(chips):
            row, device, wanted = piece_target(n, 1)

            @pl.when(jnp.logical_and(wanted, gives_bottom))
            def _():
                act(d_copy(n, jnp.maximum(c, cols_n // 2), device))

    pieces_out(lambda copy: copy.start())

    @pl.when(is_root)
    def _():
        self_copy.start()

    @pl.when(jnp.logical_and(active, jnp.logical_not(has_dn)))
    def _():
        from_below[...] = jnp.zeros_like(from_below)

    @pl.when(jnp.logical_and(active, jnp.logical_not(has_up)))
    def _():
        from_above[...] = jnp.zeros_like(from_above)
        x_l[0:2] = jnp.zeros((2, h, h), F32)
        x_l[5] = jnp.zeros((h, h), F32)

    @pl.when(jnp.logical_and(active, jnp.logical_not(has_rt)))
    def _():
        from_right[...] = jnp.zeros_like(from_right)

    @pl.when(jnp.logical_and(active, jnp.logical_not(has_lf)))
    def _():
        from_left[...] = jnp.zeros_like(from_left)

    @pl.when(jnp.logical_and(active, jnp.logical_not(has_lf)))
    def _():
        x_r[5] = jnp.zeros((h, h), F32)

    @pl.when(c == 0)
    def _():
        x_r[0:2] = jnp.zeros((2, h, h), F32)

    def y_copy(side, at_y):
        block = v_l.at[at_y]
        return remote(block, block, y_send.at[side], y_recv.at[side], y_dev[side])

    def pass_copy(side, at_y):
        block = v_l.at[at_y, :, side * 2 * piece : (side + 1) * 2 * piece]
        return remote(block, block, f_send.at[side], f_recv.at[side], y_dev[side])

    own_copy.wait()
    for d in range(3):
        z_copy(d, (zh + ZH_N - 1 - d) % ZH_N).wait_recv()
    for side in range(2):
        y_copy(side, y).start()

    tile_in.wait()

    @pl.when(active)
    def _():
        @pl.loop(0, 8)
        def _(i):
            at = pl.ds(pl.multiple_of(i * h, h), h)
            high[at, :], low[at, :] = split(tile[at, :])

    sources = (y_dn, y_up)
    for side in range(2):
        y_copy(side, sources[side]).wait_recv()
        pass_copy(side, sources[side]).start()
    far = (y + 2) % Y_N
    for side in range(2):
        pass_copy(side, far).wait_recv()

    def bottom_copy():
        return remote(v_l.at[2:4, 1], x_l.at[0:2], n_send.at[0], n_recv.at[0], dn_dev)

    def factor_copy():
        return remote(x_l.at[4], x_l.at[5], n_send.at[1], n_recv.at[1], dn_dev)

    @pl.when(has_dn)
    def _():
        bottom_copy().start()

    plan_in.wait()

    def factors(v, index, chosen):
        at_row = lax.broadcasted_iota(jnp.int32, (h, h), 0)
        at_col = lax.broadcasted_iota(jnp.int32, (h, h), 1)
        eye = jnp.where(at_row == at_col, 1.0, 0.0).astype(F32)
        powers, results, scales = [], [], []
        for k in chosen:
            panel = jnp.concatenate([v[at, k] for at in range(4)], axis=0)
            gram = exact_dot(panel.T, panel)
            upper = jnp.where(at_row < at_col, gram, jnp.where(at_row == at_col, gram * 0.5, 0.0))
            diag = jnp.where(at_row == at_col, upper, 0.0)
            power = eye - upper * (1.0 / jnp.sum(diag, axis=1, keepdims=True))
            powers.append(power)
            results.append(eye + power)
            scales.append(1.0 / jnp.sum(diag, axis=0, keepdims=True))
        span = 2
        while span < h:
            powers = [exact_dot(power, power) for power in powers]
            results = [result + exact_dot(result, power) for result, power in zip(results, powers)]
            span = span * 2
        live = [
            plan_ref[0, index] > 0,
            jnp.logical_and(plan_ref[1, index] > 0, index < rows_n - 1),
            plan_ref[2, index] > 0,
        ]
        return [jnp.where(live[k], results[n] * scales[n], 0.0) for n, k in enumerate(chosen)]

    @pl.when(active)
    def _():
        left_factors = factors(v_l, r, (0, 1, 2))
        x_l[4] = left_factors[1]
        for k in range(3):
            f_h[k], f_l[k] = split(left_factors[k].T)

    @pl.when(has_dn)
    def _():
        factor_copy().start()

    @pl.when(has_up)
    def _():
        bottom_copy().wait_recv()

    def operators(side, v, x):
        def top(k):
            return jnp.concatenate([v[0, k], v[1, k]], axis=0)

        def bottom(k):
            return jnp.concatenate([v[2, k], v[3, k]], axis=0)

        before = jnp.concatenate([x[0], x[1]], axis=0)
        pairs = [jnp.concatenate([top(0), before], axis=1), jnp.concatenate([bottom(0), top(2)], axis=1)]
        thin = [bottom(2), top(1)]
        for at in range(2):
            pair_h[2 * side + at], pair_l[2 * side + at] = split(pairs[at])
            thin_h[2 * side + at], thin_l[2 * side + at] = split(thin[at])
        first = exact_dot(before.T, top(0))
        second = exact_dot(top(2).T, bottom(0))
        cc_h[...], cc_l[...] = split(jnp.concatenate([first, second], axis=0))
        return pairs, thin

    def pair(at):
        return pair_h[at], pair_l[at]

    def thinner(at):
        return thin_h[at], thin_l[at]

    def turned(at):
        return turn_h[at], turn_l[at]

    def tthin(at):
        return tthin_h[at], tthin_l[at]

    def f_of(k):
        return f_h[k], f_l[k]

    def c_of():
        return cc_h[...], cc_l[...]

    band = [slice(i * b, (i + 1) * b) for i in range(4)]

    def band_of(i):
        return high[band[i], :], low[band[i], :]

    def lower_band(i, value):
        value = tile[band[i], :] - value
        tile[band[i], :] = value
        high[band[i], :], low[band[i], :] = split(value)

    def t_copy():
        return remote(t_own, from_above, row_send.at[0], row_recv.at[0], dn_dev)

    def p_copy():
        return remote(p_own, from_below, row_send.at[1], row_recv.at[1], up_dev)

    @pl.when(active)
    def _():
        pairs, thin = operators(0, v_l, x_l)
        for at in range(2):
            turn_h[at], turn_l[at] = split(pairs[at].T)
            tthin_h[at], tthin_l[at] = split(thin[at].T)
        t_own[...] = dot3(tthin(1), band_of(3))

    @pl.when(has_dn)
    def _():
        t_copy().start()


    @pl.when(active)
    def _():
        x0 = dot3(turned(0), band_of(0))
        x1 = dot3(turned(1), band_of(1))
        p_own[...] = x0[h:]
        t0_h[...], t0_l[...] = split(x0[:h] + x1[:h])
        t2_own[...] = x1[h:] + dot3(tthin(0), band_of(2))
        u0 = split(dot3(f_of(0), (t0_h[...], t0_l[...])))
        t0_h[...], t0_l[...] = u0
        shift = dot3(c_of(), u0)
        p_own[...] = p_own[...] - shift[:h]
        u2_h[...], u2_l[...] = split(dot3(f_of(2), split(t2_own[...] - shift[h:])))

    @pl.when(has_up)
    def _():
        p_copy().start()

    def k_copy(at):
        return remote(v_r.at[at], v_r.at[at], k_send.at[at], k_recv.at[at], core_dev)

    def l_copy():
        return remote(x_r.at[0:2], x_r.at[0:2], k_send.at[Y_N], k_recv.at[Y_N], core_dev)

    has_before = jnp.logical_and(served, c > 0)

    @pl.when(jnp.logical_and(served, first_core))
    def _():
        @pl.loop(0, Y_N)
        def _(at):
            @pl.loop(0, ZH_N)
            def _(n):
                col = at * ZH_N + n

                @pl.when(jnp.logical_or(r != c, col != c))
                def _():
                    c_copy(0, col, core_dev).wait_recv()

                @pl.when(jnp.logical_and(r == c, col == c))
                def _():
                    self_copy.wait()

            k_copy(at).start()

    @pl.when(jnp.logical_and(has_before, first_core))
    def _():
        @pl.loop(cols_n // 2, cols_n)
        def _(col):
            d_copy(0, col, core_dev).wait_recv()

        l_copy().start()


    @pl.when(has_up)
    def _():
        factor_copy().wait_recv()


    @pl.when(active)
    def _():
        u0, u2 = (t0_h[...], t0_l[...]), (u2_h[...], u2_l[...])
        lower_band(1, dot3(pair(1), join(u0, u2, 0)))
        lower_band(2, dot3(thinner(0), u2))
        f_h[3], f_l[3] = split(x_l[5].T)

    def st_copy(i):
        return remote(st_own.at[i], from_left.at[i], rt_send.at[i], rt_recv.at[i], rt_dev if i else rt_first)

    def sb_copy(i):
        return remote(sb_own.at[i], from_right.at[i], lf_send.at[i], lf_recv.at[i], lf_dev if i else lf_first)

    parts = [(slice(b, 3 * b),), (slice(0, b), slice(3 * b, 4 * b))]

    def out_copies(i):
        return [
            pltpu.make_async_copy(tile.at[at], out_ref.at[at], out_sem.at[i + n]) for n, at in enumerate(parts[i])
        ]

    def cut(i, j):
        return tuple(jnp.concatenate([ref[at, band[j]] for at in parts[i]], axis=0) for ref in (high, low))

    def lower_cols(i, j, value):
        done = 0
        for at in parts[i]:
            count = at.stop - at.start
            tile[at, band[j]] = tile[at, band[j]] - value[done : done + count]
            done = done + count

    def right_first(i):
        @pl.when(active)
        def _():
            st_own[i] = dot3(cut(i, 3), thinner(3))

        @pl.when(has_rt)
        def _():
            st_copy(i).start()

    def right_start(i):
        @pl.when(active)
        def _():
            x0 = dot3(cut(i, 0), pair(2))
            x1 = dot3(cut(i, 1), pair(3))
            y0 = split(dot3(split(x0[:, :h] + x1[:, :h]), f_of(4)))
            y0_h[i], y0_l[i] = y0
            shift = dot3(y0, c_of(), turned=True)
            sb_own[i] = x0[:, h:] - shift[:, :h]
            y2_own[...] = x1[:, h:] - shift[:, h:]

        @pl.when(has_lf)
        def _():
            sb_copy(i).start()

    def right_middle(i):
        @pl.when(active)
        def _():
            y2_of = split(dot3(split(y2_own[...] + dot3(cut(i, 2), thinner(2))), f_of(6)))
            lower_cols(i, 1, dot3(join((y0_h[i], y0_l[i]), y2_of, 1), pair(3), turned=True))
            lower_cols(i, 2, dot3(y2_of, thinner(2), turned=True))

    def right_end(i):
        @pl.when(has_rt)
        def _():
            sb_copy(i).wait_recv()

        @pl.when(has_lf)
        def _():
            st_copy(i).wait_recv()

        @pl.when(active)
        def _():
            y1 = split(dot3(split(st_own[i] + from_right[i]), f_of(5)))
            y1p = split(dot3(split(from_left[i] + sb_own[i]), f_of(7)))
            lower_cols(i, 0, dot3(join((y0_h[i], y0_l[i]), y1p, 1), pair(2), turned=True))
            lower_cols(i, 3, dot3(y1, thinner(3), turned=True))

        for copy in out_copies(i):
            copy.start()

    @pl.when(jnp.logical_and(served, jnp.logical_not(first_core)))
    def _():
        @pl.loop(0, Y_N)
        def _(at):
            k_copy(at).wait_recv()

    @pl.when(jnp.logical_and(has_before, jnp.logical_not(first_core)))
    def _():
        l_copy().wait_recv()

    def m_copy():
        return remote(x_r.at[4], x_r.at[5], m_send.at[0], m_recv.at[0], rt_dev)

    @pl.when(active)
    def _():
        operators(1, v_r, x_r)

    right_first(0)

    @pl.when(active)
    def _():
        f_h[4], f_l[4] = split(factors(v_r, c, (0,))[0])

    relay_copies = [
        (pass_rt, st_copy, remote(from_left.at[0], from_left.at[0], pass_send.at[0], rt_recv.at[0], (r, served_col + 1))),
        (pass_lf, sb_copy, remote(from_right.at[0], from_right.at[0], pass_send.at[1], lf_recv.at[0], (r, served_col - 1))),
    ]
    for there, arrived, onward in relay_copies:

        @pl.when(there)
        def _():
            arrived(0).wait_recv()
            onward.start()

    right_start(0)

    @pl.when(active)
    def _():
        second, third = factors(v_r, c, (1, 2))
        x_r[4] = second
        f_h[5], f_l[5] = split(second)
        f_h[6], f_l[6] = split(third)

    @pl.when(has_rt)
    def _():
        m_copy().start()


    @pl.when(has_dn)
    def _():
        p_copy().wait_recv()

    @pl.when(has_up)
    def _():
        t_copy().wait_recv()

    @pl.when(active)
    def _():
        u1 = split(dot3(f_of(1), split(t_own[...] + from_below[...])))
        u1p = split(dot3(f_of(3), split(from_above[...] + p_own[...])))
        lower_band(0, dot3(pair(0), join((t0_h[...], t0_l[...]), u1p, 0)))
        lower_band(3, dot3(thinner(1), u1))

    right_middle(0)
    right_first(1)
    right_start(1)
    right_middle(1)

    @pl.when(has_lf)
    def _():
        m_copy().wait_recv()

    @pl.when(active)
    def _():
        f_h[7], f_l[7] = split(x_r[5])

    right_end(0)
    right_end(1)

    for d in range(3):
        z_copy(d, zh).wait_send()
    for side in range(2):
        y_copy(side, y).wait_send()
        pass_copy(side, sources[side]).wait_send()

    @pl.when(has_dn)
    def _():
        bottom_copy().wait_send()
        factor_copy().wait_send()
        t_copy().wait_send()

    @pl.when(has_up)
    def _():
        p_copy().wait_send()

    pieces_out(lambda copy: copy.wait_send())
    for there, _, onward in relay_copies:

        @pl.when(there)
        def _():
            onward.wait_send()

    @pl.when(jnp.logical_and(served, first_core))
    def _():
        @pl.loop(0, Y_N)
        def _(at):
            k_copy(at).wait_send()

    @pl.when(jnp.logical_and(has_before, first_core))
    def _():
        l_copy().wait_send()

    @pl.when(has_rt)
    def _():
        m_copy().wait_send()

    for i in range(2):

        @pl.when(has_rt)
        def _():
            st_copy(i).wait_send()

        @pl.when(has_lf)
        def _():
            sb_copy(i).wait_send()

        for copy in out_copies(i):
            copy.wait()


def solution(mesh):
    rows_n, cols_n = mesh.shape["row"], mesh.shape["col"]

    def on_device(matrix_tiles, panels, plan):
        size, refl = matrix_tiles.shape[-1], panels.shape[-1]
        b, h = size // 4, refl
        piece = panels.shape[3]
        vmem, dma = pltpu.VMEM, pltpu.SemaphoreType.DMA
        scratch = [
            pltpu.SMEM(plan.shape, jnp.int32),
            vmem((4, 3, h, h), F32), vmem((6, h, h), F32), vmem((4, 3, h, h), F32), vmem((6, h, h), F32),
            vmem((size, size), F32), vmem((size, size), BF16), vmem((size, size), BF16),
            vmem((4, b, b), BF16), vmem((4, b, b), BF16), vmem((4, b, h), BF16), vmem((4, b, h), BF16),
            vmem((2, b, b), BF16), vmem((2, b, b), BF16), vmem((2, h, b), BF16), vmem((2, h, b), BF16),
            vmem((8, h, h), BF16), vmem((8, h, h), BF16), vmem((b, h), BF16), vmem((b, h), BF16),
            vmem((h, size), BF16), vmem((h, size), BF16), vmem((h, size), F32), vmem((h, size), BF16), vmem((h, size), BF16),
            vmem((h, size), F32), vmem((h, size), F32), vmem((h, size), F32), vmem((h, size), F32),
            vmem((2, 2 * b, h), F32), vmem((2, 2 * b, h), F32), vmem((2, 2 * b, h), F32), vmem((2, 2 * b, h), F32),
            vmem((2, 2 * b, h), BF16), vmem((2, 2 * b, h), BF16), vmem((2 * b, h), F32),
            dma((4,)), dma((3,)),
            dma((3,)), dma((3,)), dma((2,)), dma((2,)), dma((2,)), dma((2,)), dma((2,)), dma((2,)),
            dma((8,)), dma((16,)), dma((8,)), dma((8,)), dma((5,)), dma((5,)), dma((1,)), dma((1,)), dma((2,)), dma((2,)), dma((2,)), dma((2,)), dma((2,)), dma((2,)), dma((2,)),
        ]
        result = pl.pallas_call(
            functools.partial(kernel, rows_n, cols_n, b),
            out_shape=jax.ShapeDtypeStruct((size, size), F32),
            in_specs=[pl.BlockSpec(memory_space=pltpu.HBM)] * 3,
            out_specs=pl.BlockSpec(memory_space=pl.ANY),
            scratch_shapes=scratch,
            compiler_params=pltpu.CompilerParams(
                collective_id=0, has_side_effects=True, vmem_limit_bytes=48 * 1024 * 1024
            ),
        )(matrix_tiles.reshape(size, size), panels.reshape(3, piece, refl), plan)
        return result.reshape(matrix_tiles.shape)

    placed = (P(None, "row", None, "col", None, None), P(None, None, "row", "col", None), P())
    return jax.shard_map(
        on_device,
        mesh=mesh,
        in_specs=placed,
        out_specs=P(None, "row", None, "col", None, None),
        check_vma=False,
    )
```
